32 devices in a mesh: tm: 8 (over y, x, core), space: 4 (over z).
Axes of the slice: x: 2, y: 2, z: 4, core: 2. Of those that a mesh axis runs over, the one named last changes fastest.
Arguments:
- c_state: float32 [8, 3, 2, 512, 1024], P('tm', None, None, 'space'), may hold values from -4 to 4
- init: float32 [3, 2, 512, 1024], P(None, None, 'space'), may hold values from -4 to 4
Outputs:
- new_c: float32 [8, 3, 2, 512, 1024], P('tm', None, None, 'space')
- residual: float32 [8, 3, 2, 512, 1024], P('tm', None, None, 'space')
The draws below stay inside these ranges and needn't reach their ends.
All inputs are finite; a program needn't handle non-finite values.
Results may differ from the reference program's by a relative error of at most 0.00019.
Values sent between devices are 32-bit elements; how exact they have to be, the bound alone decides.
A program may use at most 128 MiB of HBM per device.

```python
import jax
import jax.numpy as jnp
from jax import lax

NG = 1024
NGH = 512
CF = 2
SLABS = 8


def shard_levels(own_key, dims, shards, smallest, largest):
    gain = 1.0
    for axis_at, parts in shards:
        draws = jax.random.uniform(jax.random.fold_in(jax.random.fold_in(own_key, 6), axis_at), (parts,), jnp.float32, smallest / len(shards), largest / len(shards))
        gain = gain * jnp.repeat(jnp.exp(draws), dims[axis_at] // parts).reshape((-1,) + (1,) * (len(dims) - 1 - axis_at))
    return gain


def gaussian(rng, extent, deviation, reach, split=(), held_as=jnp.bfloat16):
    drawn = jax.random.normal(rng, extent, jnp.float32) * deviation
    if len(split) > 0:
        drawn = shard_levels(rng, extent, split, -0.22, 0.18) * drawn
    return jnp.clip(drawn, min=-reach, max=reach).astype(held_as)


def setup_inputs(seed: int = 0) -> dict:
    seeds = jax.random.split(jax.random.key(seed), 3)
    return {
        "c_state": gaussian(seeds[0], (SLABS, 3, 2, NGH, NG), 0.5, 4.0, ((0, 8), (3, 4)), jnp.float32),
        "init": gaussian(seeds[1], (3, 2, NGH, NG), 0.5, 4.0, ((2, 4),), jnp.float32),
    }


CORIOLIS = 1.0
HYPERDIFFUSION = 0.25
COURANT = 0.4

def times_imag(values):
    return jnp.stack([-values[..., 1, :, :], values[..., 0, :, :]], axis=-3)

def divide_imag(values):
    return jnp.stack([values[..., 1, :, :], -values[..., 0, :, :]], axis=-3)

def operator_m(x_wind, y_wind, tilted, wave_x, wave_y):
    return (CORIOLIS * y_wind - wave_x * tilted, -CORIOLIS * x_wind - wave_y * tilted, wave_x * x_wind + wave_y * y_wind)

def propagate(state, steps, wave_x, wave_y, grid_size):
    time_step = COURANT / grid_size
    squared = wave_x * wave_x + wave_y * wave_y
    frequency = jnp.sqrt(CORIOLIS * CORIOLIS + squared)
    ratio = squared / (0.25 * grid_size * grid_size)
    log_damp = -HYPERDIFFUSION * (ratio * ratio) * (ratio * ratio)
    phase_angle = frequency * (steps * time_step)
    first_coef = jnp.sin(phase_angle) / frequency
    second_coef = (1.0 - jnp.cos(phase_angle)) / (frequency * frequency)
    damping = jnp.exp(steps * log_damp)
    base = (state[..., 0, :, :, :], state[..., 1, :, :, :], times_imag(state[..., 2, :, :, :]))
    applied = operator_m(base[0], base[1], base[2], wave_x, wave_y)
    applied_twice = operator_m(applied[0], applied[1], applied[2], wave_x, wave_y)
    results = [(base[field_id] + first_coef * applied[field_id] + second_coef * applied_twice[field_id]) * damping for field_id in range(3)]
    return jnp.stack([results[0], results[1], divide_imag(results[2])], axis=-4)

def wave_tables():
    counter = jnp.arange(NG, dtype=jnp.int32)
    wave_x = jnp.where(counter < NG // 2, counter, counter - NG).astype(jnp.float32)
    wave_y = jnp.arange(NGH, dtype=jnp.int32).astype(jnp.float32)[:, None]
    keep_mask = ((jnp.abs(wave_x) <= NG // 3)[None, :] & (wave_y <= NG // 3)).astype(jnp.float32)
    return (wave_x, wave_y, keep_mask)

def to_grid(coefficients):
    values = lax.complex(coefficients[:, 0], coefficients[:, 1])
    along_x = jnp.fft.ifft(values, axis=-1) * NG
    lowest = (jnp.arange(NGH, dtype=jnp.int32) == 0)[:, None]
    along_x = lax.complex(jnp.real(along_x), jnp.where(lowest, jnp.zeros_like(jnp.imag(along_x)), jnp.imag(along_x)))
    padded = jnp.concatenate([along_x, jnp.zeros_like(along_x[:, :1])], axis=1)
    return jnp.transpose(jnp.fft.irfft(padded, n=NG, axis=1), (0, 2, 1))

def to_modes(physical):
    along_y = jnp.fft.rfft(physical, axis=2)[:, :, :NGH]
    spectrum = jnp.transpose(jnp.fft.fft(along_y, axis=1) / NG, (0, 2, 1))
    return jnp.stack([jnp.real(spectrum), jnp.imag(spectrum)], axis=1)

def fine_step(state, wave_x, wave_y, keep_mask):
    time_step = COURANT / NG
    x_wind, y_wind, height = (state[0], state[1], state[2])
    vortex = times_imag(wave_x * y_wind - wave_y * x_wind)
    physical = to_grid(jnp.stack([x_wind, y_wind, height, vortex]))
    east_flow, north_flow, depth_field, spin_field = (physical[0], physical[1], physical[2], physical[3])
    products = jnp.stack([spin_field * north_flow, spin_field * east_flow, 0.5 * (east_flow * east_flow + north_flow * north_flow), depth_field * east_flow, depth_field * north_flow])
    modes = to_modes(products)
    tend_x = modes[0] - times_imag(wave_x * modes[2])
    tend_y = -modes[1] - times_imag(wave_y * modes[2])
    tend_h = -times_imag(wave_x * modes[3] + wave_y * modes[4])
    tendency = jnp.stack([tend_x, tend_y, tend_h]) * keep_mask
    return propagate(state + time_step * tendency, 1.0, wave_x, wave_y, NG)

def reference(c_state, init):
    wave_x, wave_y, keep_mask = wave_tables()
    previous = jnp.concatenate([init[None], c_state[:-1]], axis=0)

    def run_slab(start_state):
        current = start_state
        for repeat in range(CF):
            current = fine_step(current, wave_x, wave_y, keep_mask)
        return current
    ends = lax.map(run_slab, previous)
    residual = ends - c_state
    offsets = ends - propagate(previous, float(CF), wave_x, wave_y, NG)

    def advance(carried, offset):
        updated = propagate(carried, float(CF), wave_x, wave_y, NG) + offset
        return (updated, updated)
    last_state, new_c = lax.scan(advance, init, offsets)
    return (new_c, residual)
```

```python
import math

import jax
import jax.numpy as jnp
import numpy as np
from jax import lax
from jax.experimental import pallas as pl
from jax.experimental.pallas import tpu as pltpu
from jax.sharding import Mesh, PartitionSpec as P

CF = 2
CORIOLIS = 1.0
HYPERDIFFUSION = 0.25
COURANT = 0.4
RADIX = 8
ROWS = 32
SLAB = ("ta", "core")
SPACE = "sp"
EVERY = ("ta", "core", "sp")


def split_pair(values):
    high = values.astype(jnp.bfloat16)
    return high, (values - high.astype(jnp.float32)).astype(jnp.bfloat16)


def table_pair(values):
    high = lax.reduce_precision(values, 8, 7)
    return jnp.stack([high, values - high], axis=-3).astype(jnp.bfloat16)


def dot3(left, right):
    def one(a, b):
        return jnp.dot(a, b, preferred_element_type=jnp.float32)

    return one(left[0], right[0]) + (one(left[0], right[1]) + one(left[1], right[0]))


def small_fft(parts, sign):
    count = len(parts)
    if count == 1:
        return parts
    even = small_fft(parts[0::2], sign)
    odd = small_fft(parts[1::2], sign)
    low, high = [], []
    for k in range(count // 2):
        re, im = odd[k]
        if k == 0:
            tr, ti = re, im
        elif 4 * k == count:
            tr, ti = (-im, re) if sign > 0 else (im, -re)
        else:
            c = math.cos(2.0 * math.pi * k / count)
            s = sign * math.sin(2.0 * math.pi * k / count)
            tr, ti = re * c - im * s, re * s + im * c
        low.append((even[k][0] + tr, even[k][1] + ti))
        high.append((even[k][0] - tr, even[k][1] - ti))
    return low + high


def lane_tables(grid_size, sign):
    lanes = grid_size // RADIX
    n = np.arange(lanes)
    angle = 2.0 * np.pi * (n[:, None] * n[None, :] % lanes) / lanes
    c, s = np.cos(angle), sign * np.sin(angle)
    full = jnp.asarray(np.block([[c, s], [-s, c]]), jnp.float32)
    turn = 2.0 * np.pi * (np.arange(RADIX)[:, None] * n[None, :]) / grid_size
    twiddle = np.stack([np.cos(turn), sign * np.sin(turn)]).astype(np.float32)
    return table_pair(full), jnp.asarray(twiddle)


def prop_factors(steps, wave_x, wave_y, grid_size):
    time_step = COURANT / grid_size
    squared = wave_x * wave_x + wave_y * wave_y
    frequency = jnp.sqrt(CORIOLIS * CORIOLIS + squared)
    ratio = squared / (0.25 * grid_size * grid_size)
    log_damp = -HYPERDIFFUSION * (ratio * ratio) * (ratio * ratio)
    phase_angle = frequency * (steps * time_step)
    first_coef = jnp.sin(phase_angle) / frequency
    second_coef = (1.0 - jnp.cos(phase_angle)) / (frequency * frequency)
    damping = jnp.exp(steps * log_damp)
    return first_coef, second_coef, damping


def apply_parts(state, factors, kx, ky):
    first, second, damp = factors
    (xr, xi), (yr, yi), (hr, hi) = state
    done = []
    for x, y, p in ((xr, yr, -hi), (xi, yi, hr)):
        m1 = CORIOLIS * y - kx * p
        m2 = -CORIOLIS * x - ky * p
        m3 = kx * x + ky * y
        n1 = CORIOLIS * m2 - kx * m3
        n2 = -CORIOLIS * m1 - ky * m3
        n3 = kx * m1 + ky * m2
        done.append(
            (
                (x + first * m1 + second * n1) * damp,
                (y + first * m2 + second * n2) * damp,
                (p + first * m3 + second * n3) * damp,
            )
        )
    real, imag = done
    return ((real[0], imag[0]), (real[1], imag[1]), (imag[2], -real[2]))


def apply_array(state, factors, kx, ky):
    fields = tuple((state[f, 0], state[f, 1]) for f in range(3))
    made = apply_parts(fields, factors, kx, ky)
    return jnp.stack([jnp.stack(pair) for pair in made])


def waves_x(grid_size):
    counter = jnp.arange(grid_size, dtype=jnp.int32)
    return jnp.where(counter < grid_size // 2, counter, counter - grid_size).astype(jnp.float32)[None]


def row_tables(grid_size, kept):
    quarter, per = grid_size // 4, grid_size // 8
    y = jnp.arange(quarter, dtype=jnp.int32)
    q = jnp.arange(4, dtype=jnp.int32)
    ky = 4 * jnp.arange(per, dtype=jnp.int32)[None] + q[:, None]

    def waves(turns):
        angle = 2.0 * math.pi / grid_size * (turns % grid_size).astype(jnp.float32)
        return jnp.cos(angle) / grid_size, jnp.sin(angle) / grid_size

    c, s = waves(y[None, :, None] * ky[:, None, :])
    weight = jnp.where(ky == 0, 1.0, 2.0).astype(jnp.float32)[:, None, :]
    c, s = c * weight, s * weight
    inv_even = jnp.stack([jnp.concatenate([c[k], -s[k]], axis=1) for k in (0, 2)])
    inv_odd = jnp.concatenate(
        [
            jnp.concatenate([c[1], -s[1], c[3], -s[3]], axis=1),
            jnp.concatenate([s[1], c[1], -s[3], -c[3]], axis=1),
        ],
        axis=0,
    )
    c, s = waves(ky[:, :kept, None] * y[None, None, :])
    fwd_even = jnp.stack([jnp.concatenate([c[k], -s[k]], axis=0) for k in (0, 2)])
    fwd_odd = jnp.concatenate(
        [
            jnp.concatenate([c[1], -s[1]], axis=1),
            jnp.concatenate([-s[1], -c[1]], axis=1),
            jnp.concatenate([c[3], s[3]], axis=1),
            jnp.concatenate([-s[3], c[3]], axis=1),
        ],
        axis=0,
    )
    return [table_pair(t) for t in (inv_even, inv_odd, fwd_even, fwd_odd)]


def scalars(*values):
    return jnp.stack([jnp.asarray(v, jnp.int32) for v in values])


def whole_smem():
    return pl.BlockSpec(memory_space=pltpu.SMEM)


def deal(c_state, init, last, ident, group):
    _, _, _, rows, grid_size = c_state.shape
    per = rows // 4

    def kernel(at_ref, c_ref, i_ref, *refs):
        outs, held, dealt = refs[:group], refs[group], refs[group + 1]
        tile = held.shape[2]

        @pl.when(at_ref[0] > 0)
        def _():
            for n in range(held.shape[0]):
                held[n] = i_ref[0, 0, :, n * tile : (n + 1) * tile]

        @pl.when(at_ref[0] == 0)
        def _():
            for n in range(held.shape[0]):
                held[n] = c_ref[0, 0, 0, :, n * tile : (n + 1) * tile]

        for q in range(4):
            for n in range(held.shape[0]):
                dealt[q, :, n * tile : (n + 1) * tile] = held[n, pl.ds(q, per, stride=4), :]
        for turn in range(group):
            side = lax.rem(at_ref[1] + group - turn, group) // (group // 2)
            for h in range(2):
                outs[turn][h, 0, 0] = dealt[side + 2 * h]

    return pl.pallas_call(
        kernel,
        grid=(3, 2),
        in_specs=[
            whole_smem(),
            pl.BlockSpec((1, 1, 1, rows, grid_size), lambda f, c: (0, f, c, 0, 0)),
            pl.BlockSpec((1, 1, rows, grid_size), lambda f, c: (f, c, 0, 0)),
        ],
        out_specs=[pl.BlockSpec((2, 1, 1, per, grid_size), lambda f, c: (0, f, c, 0, 0))] * group,
        out_shape=[jax.ShapeDtypeStruct((2, 3, 2, per, grid_size), jnp.float32)] * group,
        scratch_shapes=[
            pltpu.VMEM((grid_size // 128, rows, 128), jnp.float32),
            pltpu.VMEM((4, per, grid_size), jnp.float32),
        ],
        name="deal",
    )(scalars(last, ident), c_state, init)


def fine_steps(landed, factors, tables, grid_size, kept, low):
    group = len(landed)
    _, _, _, short, _ = landed[0].shape
    per = grid_size // 8
    lanes = grid_size // RADIX
    half = RADIX // 2
    blocks = per // ROWS
    limit = float(grid_size // 3)
    zones = -(-(grid_size // 3 + 1) // (4 * short))
    dt = COURANT / grid_size
    inv_even, inv_odd, fwd_even, fwd_odd = tables["rows"]
    inv_x, inv_tw = tables["inv_x"]
    fwd_x, fwd_tw = tables["fwd_x"]

    def kernel(*refs):
        pieces = refs[:group]
        fac, ie, io, fe, fo, ix, itw, fx, ftw, out = refs[group : group + 10]
        state, fields, modes, delta, load, fsend, frecv, msend, mrecv = refs[group + 10 :]
        ta, me, z = (lax.axis_index(name) for name in EVERY)
        mate = (ta, 1 - me, z)
        kx = lax.broadcasted_iota(jnp.int32, (1, grid_size), 1)
        kx = jnp.where(kx < grid_size // 2, kx, kx - grid_size).astype(jnp.float32)
        slots = (2 * me, 2 - me)

        barrier = pltpu.get_barrier_semaphore()
        pl.semaphore_signal(barrier, inc=1, device_id=mate, device_id_type=pl.DeviceIdType.MESH)
        loads = []
        for n in range(group):
            at = lax.rem(n + me * (group // 2), group) * short
            loads.append(
                pltpu.make_async_copy(
                    pieces[n], state.at[:, :, :, pl.ds(pl.multiple_of(at, 8), short)], load.at[n]
                )
            )
            loads[-1].start()
        for copy in loads:
            copy.wait()
        pl.semaphore_wait(barrier, 1)

        def field_copy(b):
            h, at = b // blocks, pl.multiple_of(b % blocks * ROWS, ROWS)
            return pltpu.make_async_remote_copy(
                fields.at[2, :, h, :, pl.ds(at, ROWS)],
                fields.at[me, :, h, :, pl.ds(at, ROWS)],
                fsend.at[b],
                frecv.at[b],
                device_id=mate,
                device_id_type=pl.DeviceIdType.MESH,
            )

        def mode_copy(j):
            return pltpu.make_async_remote_copy(
                modes.at[2, j],
                modes.at[me, j],
                msend.at[j],
                mrecv.at[j],
                device_id=mate,
                device_id_type=pl.DeviceIdType.MESH,
            )

        def rows_ky(h, at, count):
            m = lax.broadcasted_iota(jnp.int32, (count, 1), 0) + at
            return (4 * m + 2 * h + me).astype(jnp.float32)

        def inverse(b, carry):
            h, at = b // blocks, pl.multiple_of(b % blocks * ROWS, ROWS)
            ky = rows_ky(h, at, ROWS)
            row = pl.ds(at, ROWS)
            for f in range(4):
                if f < 3:
                    re, im = state[h, f, 0, row], state[h, f, 1, row]
                else:
                    re = ky * state[h, 0, 1, row] - kx * state[h, 1, 1, row]
                    im = kx * state[h, 1, 0, row] - ky * state[h, 0, 0, row]
                parts = [
                    (re[:, n * lanes : (n + 1) * lanes], im[:, n * lanes : (n + 1) * lanes])
                    for n in range(RADIX)
                ]
                turned = []
                for k, (a, b_) in enumerate(small_fft(parts, 1.0)):
                    if k > 0:
                        c, s = itw[0, k : k + 1], itw[1, k : k + 1]
                        a, b_ = a * c - b_ * s, a * s + b_ * c
                    turned.append(jnp.concatenate([a, b_], axis=1))
                made = dot3(split_pair(jnp.concatenate(turned, axis=0)), (ix[0], ix[1]))
                for k in range(RADIX):
                    for c in range(2):
                        fields[slots[k // half], k % half, h, c, row, f * lanes : (f + 1) * lanes] = made[
                            k * ROWS : (k + 1) * ROWS, c * lanes : (c + 1) * lanes
                        ]
            field_copy(b).start()
            return carry

        def middle(j, carry):
            def rows(c, h):
                return fields[c, j, h].reshape(2 * per, 4 * lanes)

            even = dot3((ie[0, 0], ie[0, 1]), split_pair(rows(0, 0)))
            other = dot3((ie[1, 0], ie[1, 1]), split_pair(rows(0, 1)))
            odd = dot3(
                (io[0], io[1]), split_pair(jnp.concatenate([rows(1, 0), rows(1, 1)], axis=0))
            )
            re, im = odd[: 2 * per], odd[2 * per :]
            plus, minus = even + other, even - other
            made = []
            for grid in (plus + re, minus - im, plus - re, minus + im):
                u, v, h, w = (grid[:, f * lanes : (f + 1) * lanes] for f in range(4))
                made.append(
                    jnp.concatenate([w * v, w * u, 0.5 * (u * u + v * v), h * u, h * v], axis=1)
                )
            a, b = made[0] + made[2], made[1] + made[3]
            for h, term in enumerate((a + b, a - b)):
                got = dot3((fe[h, 0], fe[h, 1]), split_pair(term))
                modes[slots[0], j, h] = got.reshape(2, kept, 5 * lanes)
            term = jnp.concatenate([made[0] - made[2], made[1] - made[3]], axis=0)
            got = dot3((fo[0], fo[1]), split_pair(term))
            for h in range(2):
                modes[slots[1], j, h] = got[2 * kept * h : 2 * kept * (h + 1)].reshape(
                    2, kept, 5 * lanes
                )
            mode_copy(j).start()
            return carry

        def read(ref, at):
            return tuple(
                tuple(
                    jnp.concatenate([ref[h, f, c, pl.ds(at, 8)] for h in range(2)], axis=0)
                    for c in range(2)
                )
                for f in range(3)
            )

        def write(ref, at, values):
            for f in range(3):
                for c in range(2):
                    for h in range(2):
                        ref[h, f, c, pl.ds(at, 8)] = values[f][c][8 * h : 8 * h + 8]

        def rows_of(i):
            at = pl.multiple_of(i * 8, 8)
            ky = jnp.concatenate([rows_ky(h, at, 8) for h in range(2)], axis=0)
            factors = tuple(
                jnp.concatenate([fac[n, h, pl.ds(at, 8)] for h in range(2)], axis=0) for n in range(3)
            )
            return at, ky, factors

        def plain(i, carry):
            at, ky, factors = rows_of(i)
            write(state, at, apply_parts(read(state, at), factors, kx, ky))
            return carry

        def forward(step):
            def body(i, carry):
                at, ky, factors = rows_of(i)

                def piece(f, c, k):
                    return jnp.concatenate(
                        [
                            modes[k // half, k % half, h, c, pl.ds(at, 8), f * lanes : (f + 1) * lanes]
                            for h in range(2)
                        ],
                        axis=0,
                    )

                stacked = jnp.concatenate(
                    [
                        jnp.concatenate([piece(f, 0, k), piece(f, 1, k)], axis=1)
                        for f in range(5)
                        for k in range(RADIX)
                    ],
                    axis=0,
                )
                made = dot3(split_pair(stacked), (fx[0], fx[1]))
                found = []
                for f in range(5):
                    parts = []
                    for k in range(RADIX):
                        start = (f * RADIX + k) * 16
                        a = made[start : start + 16, :lanes]
                        b = made[start : start + 16, lanes:]
                        if k > 0:
                            c, s = ftw[0, k : k + 1], ftw[1, k : k + 1]
                            a, b = a * c - b * s, a * s + b * c
                        parts.append((a, b))
                    parts = small_fft(parts, -1.0)
                    found.append(
                        tuple(jnp.concatenate([p[c] for p in parts], axis=1) for c in range(2))
                    )
                (ar, ai), (br, bi), (kr, ki), (pr, pi), (qr, qi) = found
                inside = (jnp.abs(kx) <= limit) & (ky <= limit)

                def keep(values):
                    return jnp.where(inside, dt * values, 0.0)

                change = (
                    (keep(ar + kx * ki), keep(ai - kx * kr)),
                    (keep(ky * ki - br), -keep(bi + ky * kr)),
                    (keep(kx * pi + ky * qi), -keep(kx * pr + ky * qr)),
                )

                def add(left, right):
                    return tuple(tuple(a + b for a, b in zip(p, q)) for p, q in zip(left, right))

                if step == 0:
                    change = apply_parts(change, factors, kx, ky)
                    write(delta, at, change)
                    moved = apply_parts(read(state, at), factors, kx, ky)
                    write(state, at, add(moved, change))
                else:
                    change = add(change, read(delta, at))
                    change = apply_parts(change, factors, kx, ky)
                    zone = at // short
                    inner = pl.multiple_of(lax.rem(at, short), 8)
                    for f in range(3):
                        for c in range(2):
                            for h in range(2):
                                value = change[f][c][8 * h : 8 * h + 8]
                                out[zone, h, f, c, pl.ds(inner, 8), :low] = value[:, :low]
                                out[zone, h, f, c, pl.ds(inner, 8), low:] = value[:, grid_size - low :]
                return carry

            return body

        for step in range(CF):
            lax.fori_loop(0, 2 * blocks, inverse, 0)
            for b in range(2 * blocks):
                field_copy(b).wait()
            lax.fori_loop(0, half, middle, 0)
            if step < CF - 1:
                lax.fori_loop(kept // 8, per // 8, plain, 0)
            for j in range(half):
                mode_copy(j).wait()
            lax.fori_loop(0, kept // 8, forward(step), 0)
        if kept < zones * short:
            for h in range(2):
                for f in range(3):
                    for c in range(2):
                        start = kept - (zones - 1) * short
                        out[zones - 1, h, f, c, start:] = jnp.zeros((short - start, 2 * low), jnp.float32)

    ops = [factors, inv_even, inv_odd, fwd_even, fwd_odd, inv_x, inv_tw, fwd_x, fwd_tw]
    return pl.pallas_call(
        kernel,
        in_specs=[pl.BlockSpec(memory_space=pl.ANY)] * group
        + [pl.BlockSpec(memory_space=pltpu.VMEM)] * len(ops),
        out_specs=pl.BlockSpec(memory_space=pltpu.VMEM),
        out_shape=jax.ShapeDtypeStruct((zones, 2, 3, 2, short, 2 * low), jnp.float32),
        scratch_shapes=[
            pltpu.VMEM((2, 3, 2, per, grid_size), jnp.float32),
            pltpu.VMEM((3, half, 2, 2, per, 4 * lanes), jnp.float32),
            pltpu.VMEM((3, half, 2, 2, kept, 5 * lanes), jnp.float32),
            pltpu.VMEM((2, 3, 2, kept, grid_size), jnp.float32),
            pltpu.SemaphoreType.DMA((group,)),
            pltpu.SemaphoreType.DMA((2 * blocks,)),
            pltpu.SemaphoreType.DMA((2 * blocks,)),
            pltpu.SemaphoreType.DMA((half,)),
            pltpu.SemaphoreType.DMA((half,)),
        ],
        compiler_params=pltpu.CompilerParams(
            collective_id=0, has_side_effects=True, vmem_limit_bytes=62 * 1024 * 1024
        ),
        name="fine_steps",
    )(*landed, *ops)


def slab_scan(data, factors, kx, ky):
    def kernel(data_ref, fac_ref, kx_ref, ky_ref, out_ref):
        kx, ky = kx_ref[...], ky_ref[...]
        factors = (fac_ref[0], fac_ref[1], fac_ref[2])
        carried = None
        for k in range(data_ref.shape[0]):
            new = tuple((data_ref[k, f, 0], data_ref[k, f, 1]) for f in range(3))
            if carried is not None:
                moved = apply_parts(carried, factors, kx, ky)
                new = tuple((moved[f][0] + new[f][0], moved[f][1] + new[f][1]) for f in range(3))
            for f in range(3):
                for c in range(2):
                    out_ref[k, f, c] = new[f][c]
            carried = new

    slabs, _, _, rows, width = data.shape
    return pl.pallas_call(
        kernel,
        grid=(width // 128,),
        in_specs=[
            pl.BlockSpec((slabs, 3, 2, rows, 128), lambda i: (0, 0, 0, 0, i)),
            pl.BlockSpec((3, rows, 128), lambda i: (0, 0, i)),
            pl.BlockSpec((1, 128), lambda i: (0, i)),
            pl.BlockSpec((rows, 1), lambda i: (0, 0)),
        ],
        out_specs=pl.BlockSpec((slabs, 3, 2, rows, 128), lambda i: (0, 0, 0, 0, i)),
        out_shape=jax.ShapeDtypeStruct(data.shape, jnp.float32),
        name="slab_scan",
    )(data, factors, kx, ky)


def shards(c_state, init):
    rows, grid_size = c_state.shape[3:]
    group = lax.axis_size(SPACE)
    slabs = lax.axis_size(SLAB)
    slab = lax.axis_index(SLAB)
    core = lax.axis_index("core")
    zone = lax.axis_index(SPACE)
    short = rows // 4
    limit = grid_size // 3
    zones = -(-(limit + 1) // rows)
    kept = -(-(limit // 4 + 1) // 8) * 8
    low = (limit // 128 + 1) * 128
    where = (group // 2 - 1, group // 2)

    def device(k, z):
        return k * group + z

    pieces = deal(c_state, init, slab == slabs - 1, zone, group)
    landed = []
    for n, piece in enumerate(pieces):
        links = [
            (device(k, (n + c * (group // 2)) % group), device(k // 2 * 2 + c, where[k % 2]))
            for k in range(slabs)
            for c in range(2)
        ]
        landed.append(lax.ppermute(piece, EVERY, links))
    links = [(device(k, z), device(k + 1, z)) for k in range(slabs - 1) for z in range(group)]
    before = jnp.where(slab == 0, init, lax.ppermute(c_state[0], EVERY, links))

    kx = waves_x(grid_size)
    tables = {
        "rows": row_tables(grid_size, kept),
        "inv_x": lane_tables(grid_size, 1.0),
        "fwd_x": lane_tables(grid_size, -1.0),
    }
    ky = 4 * jnp.arange(grid_size // 8, dtype=jnp.int32)[None] + 2 * jnp.arange(2, dtype=jnp.int32)[:, None]
    ky = (ky + core).astype(jnp.float32)[:, :, None]
    factors = jnp.stack(prop_factors(1.0, kx[None], ky, grid_size))

    ky = (zone * rows + jnp.arange(rows, dtype=jnp.int32)).astype(jnp.float32)[:, None]
    first = apply_array(init, prop_factors((CF * (slab + 1)).astype(jnp.float32), kx, ky, grid_size), kx, ky)
    second = apply_array(before, prop_factors(float(CF), kx, ky, grid_size), kx, ky) - c_state[0]
    landed, factors, tables, first, second = lax.optimization_barrier((landed, factors, tables, first, second))
    made = fine_steps(landed, factors, tables, grid_size, kept, low)

    got = []
    for n in range(zones):
        piece = lax.dynamic_index_in_dim(made, (n + core) % zones, 0, keepdims=False)
        links = [
            (device(k // 2 * 2 + c, where[k % 2]), device((k + 1) % slabs, (n + c) % zones))
            for k in range(slabs)
            for c in range(2)
        ]
        got.append(lax.ppermute(piece, EVERY, links))
    got = jnp.stack(got)
    sides = [lax.dynamic_index_in_dim(got, (zone + zones - c) % zones, 0, keepdims=False) for c in range(2)]
    off = jnp.stack(sides, axis=-3).transpose(1, 2, 4, 0, 3, 5).reshape(3, 2, short, 4, 2 * low)
    off = jnp.where(zone < zones, off.reshape(3, 2, rows, 2 * low), 0.0)

    per = rows // slabs
    kx_low = jnp.concatenate([kx[:, :low], kx[:, grid_size - low :]], axis=1)
    start = zone * rows + slab * per
    ky = (start + jnp.arange(per, dtype=jnp.int32)).astype(jnp.float32)[:, None]
    coarse = jnp.stack(prop_factors(float(CF), kx_low, ky, grid_size))
    split = off.reshape(3, 2, slabs, per, 2 * low).transpose(2, 0, 1, 3, 4)
    split = lax.all_to_all(split, SLAB, split_axis=0, concat_axis=0, tiled=True)
    split = slab_scan(split, coarse, kx_low, ky)
    split = lax.all_to_all(split, SLAB, split_axis=0, concat_axis=0, tiled=True)
    moved = split.transpose(1, 2, 0, 3, 4).reshape(off.shape)

    def widen(base, extra):
        return jnp.concatenate(
            [
                base[..., :low] + extra[..., :low],
                base[..., low : grid_size - low],
                base[..., grid_size - low :] + extra[..., low:],
            ],
            axis=-1,
        )

    return widen(first, moved)[None], widen(second, off)[None]


def solution(mesh):
    slabs, space = mesh.devices.shape
    fine = Mesh(mesh.devices.reshape(slabs // 2, 2, space), EVERY)
    spec = P(SLAB, None, None, SPACE, None)
    return jax.shard_map(
        shards,
        mesh=fine,
        in_specs=(spec, P(None, None, SPACE, None)),
        out_specs=(spec, spec),
        check_vma=False,
    )
```

```python
import math

import jax
import jax.numpy as jnp
import numpy as np
from jax import lax
from jax.experimental import pallas as pl
from jax.experimental.pallas import tpu as pltpu
from jax.sharding import Mesh, PartitionSpec as P

CF = 2
CORIOLIS = 1.0
HYPERDIFFUSION = 0.25
COURANT = 0.4
RADIX = 8
ROWS = 32
SLAB = ("ta", "core")
SPACE = "sp"
EVERY = ("ta", "core", "sp")


def split_pair(values):
    high = values.astype(jnp.bfloat16)
    return high, (values - high.astype(jnp.float32)).astype(jnp.bfloat16)


def table_pair(values):
    high = lax.reduce_precision(values, 8, 7)
    return jnp.stack([high, values - high], axis=-3).astype(jnp.bfloat16)


def dot3(left, right):
    def one(a, b):
        return jnp.dot(a, b, preferred_element_type=jnp.float32)

    return one(left[0], right[0]) + (one(left[0], right[1]) + one(left[1], right[0]))


def small_fft(parts, sign):
    count = len(parts)
    if count == 1:
        return parts
    even = small_fft(parts[0::2], sign)
    odd = small_fft(parts[1::2], sign)
    low, high = [], []
    for k in range(count // 2):
        re, im = odd[k]
        if k == 0:
            tr, ti = re, im
        elif 4 * k == count:
            tr, ti = (-im, re) if sign > 0 else (im, -re)
        else:
            c = math.cos(2.0 * math.pi * k / count)
            s = sign * math.sin(2.0 * math.pi * k / count)
            tr, ti = re * c - im * s, re * s + im * c
        low.append((even[k][0] + tr, even[k][1] + ti))
        high.append((even[k][0] - tr, even[k][1] - ti))
    return low + high


def lane_tables(grid_size, sign):
    lanes = grid_size // RADIX
    n = np.arange(lanes)
    angle = 2.0 * np.pi * (n[:, None] * n[None, :] % lanes) / lanes
    c, s = np.cos(angle), sign * np.sin(angle)
    full = jnp.asarray(np.block([[c, s], [-s, c]]), jnp.float32)
    turn = 2.0 * np.pi * (np.arange(RADIX)[:, None] * n[None, :]) / grid_size
    twiddle = np.stack([np.cos(turn), sign * np.sin(turn)]).astype(np.float32)
    return table_pair(full), jnp.asarray(twiddle)


def prop_factors(steps, wave_x, wave_y, grid_size):
    time_step = COURANT / grid_size
    squared = wave_x * wave_x + wave_y * wave_y
    frequency = jnp.sqrt(CORIOLIS * CORIOLIS + squared)
    ratio = squared / (0.25 * grid_size * grid_size)
    log_damp = -HYPERDIFFUSION * (ratio * ratio) * (ratio * ratio)
    phase_angle = frequency * (steps * time_step)
    first_coef = jnp.sin(phase_angle) / frequency
    second_coef = (1.0 - jnp.cos(phase_angle)) / (frequency * frequency)
    damping = jnp.exp(steps * log_damp)
    return first_coef, second_coef, damping


def apply_parts(state, factors, kx, ky):
    first, second, damp = factors
    (xr, xi), (yr, yi), (hr, hi) = state
    done = []
    for x, y, p in ((xr, yr, -hi), (xi, yi, hr)):
        m1 = CORIOLIS * y - kx * p
        m2 = -CORIOLIS * x - ky * p
        m3 = kx * x + ky * y
        n1 = CORIOLIS * m2 - kx * m3
        n2 = -CORIOLIS * m1 - ky * m3
        n3 = kx * m1 + ky * m2
        done.append(
            (
                (x + first * m1 + second * n1) * damp,
                (y + first * m2 + second * n2) * damp,
                (p + first * m3 + second * n3) * damp,
            )
        )
    real, imag = done
    return ((real[0], imag[0]), (real[1], imag[1]), (imag[2], -real[2]))


def apply_array(state, factors, kx, ky):
    fields = tuple((state[f, 0], state[f, 1]) for f in range(3))
    made = apply_parts(fields, factors, kx, ky)
    return jnp.stack([jnp.stack(pair) for pair in made])


def waves_x(grid_size):
    counter = jnp.arange(grid_size, dtype=jnp.int32)
    return jnp.where(counter < grid_size // 2, counter, counter - grid_size).astype(jnp.float32)[None]


def row_tables(grid_size, kept):
    quarter, per = grid_size // 4, grid_size // 8
    y = jnp.arange(quarter, dtype=jnp.int32)
    q = jnp.arange(4, dtype=jnp.int32)
    ky = 4 * jnp.arange(per, dtype=jnp.int32)[None] + q[:, None]

    def waves(turns):
        angle = 2.0 * math.pi / grid_size * (turns % grid_size).astype(jnp.float32)
        return jnp.cos(angle) / grid_size, jnp.sin(angle) / grid_size

    c, s = waves(y[None, :, None] * ky[:, None, :])
    weight = jnp.where(ky == 0, 1.0, 2.0).astype(jnp.float32)[:, None, :]
    c, s = c * weight, s * weight
    inv_even = jnp.stack([jnp.concatenate([c[k], -s[k]], axis=1) for k in (0, 2)])
    inv_odd = jnp.concatenate(
        [
            jnp.concatenate([c[1], -s[1], c[3], -s[3]], axis=1),
            jnp.concatenate([s[1], c[1], -s[3], -c[3]], axis=1),
        ],
        axis=0,
    )
    c, s = waves(ky[:, :kept, None] * y[None, None, :])
    fwd_even = jnp.stack([jnp.concatenate([c[k], -s[k]], axis=0) for k in (0, 2)])
    fwd_odd = jnp.concatenate(
        [
            jnp.concatenate([c[1], -s[1]], axis=1),
            jnp.concatenate([-s[1], -c[1]], axis=1),
            jnp.concatenate([c[3], s[3]], axis=1),
            jnp.concatenate([-s[3], c[3]], axis=1),
        ],
        axis=0,
    )
    return [table_pair(t) for t in (inv_even, inv_odd, fwd_even, fwd_odd)]


def scalars(*values):
    return jnp.stack([jnp.asarray(v, jnp.int32) for v in values])


def whole_smem():
    return pl.BlockSpec(memory_space=pltpu.SMEM)


def deal(c_state, init, last, ident, group):
    _, _, _, rows, grid_size = c_state.shape
    per = rows // 4

    def kernel(at_ref, c_ref, i_ref, *refs):
        outs, held, dealt = refs[:group], refs[group], refs[group + 1]
        tile = held.shape[2]

        @pl.when(at_ref[0] > 0)
        def _():
            for n in range(held.shape[0]):
                held[n] = i_ref[0, 0, :, n * tile : (n + 1) * tile]

        @pl.when(at_ref[0] == 0)
        def _():
            for n in range(held.shape[0]):
                held[n] = c_ref[0, 0, 0, :, n * tile : (n + 1) * tile]

        for q in range(4):
            for n in range(held.shape[0]):
                dealt[q, :, n * tile : (n + 1) * tile] = held[n, pl.ds(q, per, stride=4), :]
        for turn in range(group):
            side = lax.rem(at_ref[1] + group - turn, group) // (group // 2)
            for h in range(2):
                outs[turn][h, 0, 0] = dealt[side + 2 * h]

    return pl.pallas_call(
        kernel,
        grid=(3, 2),
        in_specs=[
            whole_smem(),
            pl.BlockSpec((1, 1, 1, rows, grid_size), lambda f, c: (0, f, c, 0, 0)),
            pl.BlockSpec((1, 1, rows, grid_size), lambda f, c: (f, c, 0, 0)),
        ],
        out_specs=[pl.BlockSpec((2, 1, 1, per, grid_size), lambda f, c: (0, f, c, 0, 0))] * group,
        out_shape=[jax.ShapeDtypeStruct((2, 3, 2, per, grid_size), jnp.float32)] * group,
        scratch_shapes=[
            pltpu.VMEM((grid_size // 128, rows, 128), jnp.float32),
            pltpu.VMEM((4, per, grid_size), jnp.float32),
        ],
        name="deal",
    )(scalars(last, ident), c_state, init)


def fine_steps(landed, factors, scan_factors, tables, grid_size, kept, low, slabs, where):
    group = len(landed)
    chips = slabs // 2
    MESH = pl.DeviceIdType.MESH
    _, _, _, short, _ = landed[0].shape
    per = grid_size // 8
    lanes = grid_size // RADIX
    half = RADIX // 2
    blocks = per // ROWS
    limit = float(grid_size // 3)
    zones = -(-(grid_size // 3 + 1) // (4 * short))
    dt = COURANT / grid_size
    total = kept // 8
    each = short // 8
    inv_even, inv_odd, fwd_even, fwd_odd = tables["rows"]
    inv_x, inv_tw = tables["inv_x"]
    fwd_x, fwd_tw = tables["fwd_x"]

    def kernel(*refs):
        pieces = refs[:group]
        fac, sfac, ie, io, fe, fo, ix, itw, fx, ftw, off_out, sum_out = refs[group : group + 12]
        state, fields, modes, delta, sent, off, mates, carry_in, sums = refs[group + 12 : group + 21]
        load, fsend, frecv, msend, mrecv, bsend, brecv, psend, precv, csend, crecv, ssend, srecv, osem, usem = refs[
            group + 21 :
        ]
        ta, me, z = (lax.axis_index(name) for name in EVERY)
        mate = (ta, 1 - me, z)
        is_job = (z == where[0]) | (z == where[1])
        is_home = z < zones
        first = ta == 0
        passes_on = (me == 1) & (ta < chips - 1) & is_home
        slab = 2 * ta + jnp.where(z == where[1], 1, 0)
        target = lax.rem(slab + 1, slabs)
        own = 2 * ta + me
        source = lax.rem(own + slabs - 1, slabs)
        source_z = jnp.where(lax.rem(source, 2) == 1, where[1], where[0])
        home_is_own = (target == own) & is_job & is_home
        kx = lax.broadcasted_iota(jnp.int32, (1, grid_size), 1)
        kx = jnp.where(kx < grid_size // 2, kx, kx - grid_size).astype(jnp.float32)
        slots = (2 * me, 2 - me)

        barrier = pltpu.get_barrier_semaphore()
        pl.semaphore_signal(barrier, inc=1, device_id=mate, device_id_type=MESH)
        for side in range(2):
            job = (source // 2, side, source_z)
            is_self = (source // 2 == ta) & (source_z == z) & (me == side)

            @pl.when(is_home & jnp.logical_not(is_self))
            def _():
                pl.semaphore_signal(barrier, inc=1, device_id=job, device_id_type=MESH)

        @pl.when(is_home & (me == 1) & (ta > 0))
        def _():
            pl.semaphore_signal(barrier, inc=1, device_id=(ta - 1, me, z), device_id_type=MESH)

        loads = []
        for n in range(group):
            at = lax.rem(n + me * (group // 2), group) * short
            loads.append(
                pltpu.make_async_copy(
                    pieces[n], state.at[:, :, :, pl.ds(pl.multiple_of(at, 8), short)], load.at[n]
                )
            )
            loads[-1].start()
        for copy in loads:
            copy.wait()
        expected = 1 + jnp.where(is_job, zones, 0) - jnp.where(home_is_own, 1, 0) + jnp.where(passes_on, 1, 0)
        pl.semaphore_wait(barrier, expected)

        def back_copy(i):
            return pltpu.make_async_remote_copy(
                sent.at[i],
                off.at[me, lax.rem(i, each)],
                bsend.at[i],
                brecv.at[me, lax.rem(i, each)],
                device_id=(target // 2, lax.rem(target, 2), i // each),
                device_id_type=MESH,
            )

        def stays(i):
            return home_is_own & (i // each == z)

        def field_copy(b):
            h, at = b // blocks, pl.multiple_of(b % blocks * ROWS, ROWS)
            return pltpu.make_async_remote_copy(
                fields.at[2, :, h, :, pl.ds(at, ROWS)],
                fields.at[me, :, h, :, pl.ds(at, ROWS)],
                fsend.at[b],
                frecv.at[b],
                device_id=mate,
                device_id_type=pl.DeviceIdType.MESH,
            )

        def mode_copy(j):
            return pltpu.make_async_remote_copy(
                modes.at[2, j],
                modes.at[me, j],
                msend.at[j],
                mrecv.at[j],
                device_id=mate,
                device_id_type=pl.DeviceIdType.MESH,
            )

        def rows_ky(h, at, count):
            m = lax.broadcasted_iota(jnp.int32, (count, 1), 0) + at
            return (4 * m + 2 * h + me).astype(jnp.float32)

        def inverse(b, carry):
            h, at = b // blocks, pl.multiple_of(b % blocks * ROWS, ROWS)
            ky = rows_ky(h, at, ROWS)
            row = pl.ds(at, ROWS)
            for f in range(4):
                if f < 3:
                    re, im = state[h, f, 0, row], state[h, f, 1, row]
                else:
                    re = ky * state[h, 0, 1, row] - kx * state[h, 1, 1, row]
                    im = kx * state[h, 1, 0, row] - ky * state[h, 0, 0, row]
                parts = [
                    (re[:, n * lanes : (n + 1) * lanes], im[:, n * lanes : (n + 1) * lanes])
                    for n in range(RADIX)
                ]
                turned = []
                for k, (a, b_) in enumerate(small_fft(parts, 1.0)):
                    if k > 0:
                        c, s = itw[0, k : k + 1], itw[1, k : k + 1]
                        a, b_ = a * c - b_ * s, a * s + b_ * c
                    turned.append(jnp.concatenate([a, b_], axis=1))
                made = dot3(split_pair(jnp.concatenate(turned, axis=0)), (ix[0], ix[1]))
                for k in range(RADIX):
                    for c in range(2):
                        fields[slots[k // half], k % half, h, c, row, f * lanes : (f + 1) * lanes] = made[
                            k * ROWS : (k + 1) * ROWS, c * lanes : (c + 1) * lanes
                        ]
            field_copy(b).start()
            return carry

        def middle(j, carry):
            def rows(c, h):
                return fields[c, j, h].reshape(2 * per, 4 * lanes)

            even = dot3((ie[0, 0], ie[0, 1]), split_pair(rows(0, 0)))
            other = dot3((ie[1, 0], ie[1, 1]), split_pair(rows(0, 1)))
            odd = dot3(
                (io[0], io[1]), split_pair(jnp.concatenate([rows(1, 0), rows(1, 1)], axis=0))
            )
            re, im = odd[: 2 * per], odd[2 * per :]
            plus, minus = even + other, even - other
            made = []
            for grid in (plus + re, minus - im, plus - re, minus + im):
                u, v, h, w = (grid[:, f * lanes : (f + 1) * lanes] for f in range(4))
                made.append(
                    jnp.concatenate([w * v, w * u, 0.5 * (u * u + v * v), h * u, h * v], axis=1)
                )
            a, b = made[0] + made[2], made[1] + made[3]
            for h, term in enumerate((a + b, a - b)):
                got = dot3((fe[h, 0], fe[h, 1]), split_pair(term))
                modes[slots[0], j, h] = got.reshape(2, kept, 5 * lanes)
            term = jnp.concatenate([made[0] - made[2], made[1] - made[3]], axis=0)
            got = dot3((fo[0], fo[1]), split_pair(term))
            for h in range(2):
                modes[slots[1], j, h] = got[2 * kept * h : 2 * kept * (h + 1)].reshape(
                    2, kept, 5 * lanes
                )
            mode_copy(j).start()
            return carry

        def read(ref, at):
            return tuple(
                tuple(
                    jnp.concatenate([ref[h, f, c, pl.ds(at, 8)] for h in range(2)], axis=0)
                    for c in range(2)
                )
                for f in range(3)
            )

        def write(ref, at, values):
            for f in range(3):
                for c in range(2):
                    for h in range(2):
                        ref[h, f, c, pl.ds(at, 8)] = values[f][c][8 * h : 8 * h + 8]

        def rows_of(i):
            at = pl.multiple_of(i * 8, 8)
            ky = jnp.concatenate([rows_ky(h, at, 8) for h in range(2)], axis=0)
            factors = tuple(
                jnp.concatenate([fac[n, h, pl.ds(at, 8)] for h in range(2)], axis=0) for n in range(3)
            )
            return at, ky, factors

        def plain(i, carry):
            at, ky, factors = rows_of(i)
            write(state, at, apply_parts(read(state, at), factors, kx, ky))
            return carry

        def forward(step):
            def body(i, carry):
                at, ky, factors = rows_of(i)

                def piece(f, c, k):
                    return jnp.concatenate(
                        [
                            modes[k // half, k % half, h, c, pl.ds(at, 8), f * lanes : (f + 1) * lanes]
                            for h in range(2)
                        ],
                        axis=0,
                    )

                stacked = jnp.concatenate(
                    [
                        jnp.concatenate([piece(f, 0, k), piece(f, 1, k)], axis=1)
                        for f in range(5)
                        for k in range(RADIX)
                    ],
                    axis=0,
                )
                made = dot3(split_pair(stacked), (fx[0], fx[1]))
                found = []
                for f in range(5):
                    parts = []
                    for k in range(RADIX):
                        start = (f * RADIX + k) * 16
                        a = made[start : start + 16, :lanes]
                        b = made[start : start + 16, lanes:]
                        if k > 0:
                            c, s = ftw[0, k : k + 1], ftw[1, k : k + 1]
                            a, b = a * c - b * s, a * s + b * c
                        parts.append((a, b))
                    parts = small_fft(parts, -1.0)
                    found.append(
                        tuple(jnp.concatenate([p[c] for p in parts], axis=1) for c in range(2))
                    )
                (ar, ai), (br, bi), (kr, ki), (pr, pi), (qr, qi) = found
                inside = (jnp.abs(kx) <= limit) & (ky <= limit)

                def keep(values):
                    return jnp.where(inside, dt * values, 0.0)

                change = (
                    (keep(ar + kx * ki), keep(ai - kx * kr)),
                    (keep(ky * ki - br), -keep(bi + ky * kr)),
                    (keep(kx * pi + ky * qi), -keep(kx * pr + ky * qr)),
                )

                def add(left, right):
                    return tuple(tuple(a + b for a, b in zip(p, q)) for p, q in zip(left, right))

                if step == 0:
                    change = apply_parts(change, factors, kx, ky)
                    write(delta, at, change)
                    moved = apply_parts(read(state, at), factors, kx, ky)
                    write(state, at, add(moved, change))
                else:
                    change = add(change, read(delta, at))
                    change = apply_parts(change, factors, kx, ky)
                    for f in range(3):
                        for c in range(2):
                            for h in range(2):
                                value = change[f][c][8 * h : 8 * h + 8]
                                sent[i, h, f, c, :, :low] = value[:, :low]
                                sent[i, h, f, c, :, low:] = value[:, grid_size - low :]

                    @pl.when(stays(i))
                    def _():
                        at = lax.rem(i, each)
                        pltpu.make_async_copy(sent.at[i], off.at[me, at], brecv.at[me, at]).start()

                    @pl.when(is_job & jnp.logical_not(stays(i)))
                    def _():
                        back_copy(i).start()

                return carry

            return body

        for step in range(CF):
            lax.fori_loop(0, 2 * blocks, inverse, 0)
            for b in range(2 * blocks):
                field_copy(b).wait()
            lax.fori_loop(0, half, middle, 0)
            if step < CF - 1:
                lax.fori_loop(kept // 8, per // 8, plain, 0)
            for j in range(half):
                mode_copy(j).wait()
            lax.fori_loop(0, kept // 8, forward(step), 0)

        kx_low = jnp.concatenate([kx[:, :low], kx[:, grid_size - low :]], axis=1)

        def chunk(ref, side, at):
            return tuple(
                tuple(jnp.concatenate([ref[side, at, h, f, c] for h in range(2)], axis=0) for c in range(2))
                for f in range(3)
            )

        def moved(n, values, side, at):
            m = lax.broadcasted_iota(jnp.int32, (8, 1), 0) + (z * short + at * 8)
            ky = jnp.concatenate([4 * m + 2 * h + side for h in range(2)], axis=0).astype(jnp.float32)
            factors = tuple(
                jnp.concatenate([sfac[n, k, side, at, h] for h in range(2)], axis=0) for k in range(3)
            )
            return apply_parts(values, factors, kx_low, ky)

        def put(side, at, values):
            for f in range(3):
                for c in range(2):
                    for h in range(2):
                        sums[side, at, h, f, c] = values[f][c][8 * h : 8 * h + 8]
            pltpu.make_async_copy(sums.at[side, at], sum_out.at[side, at], usem.at[side, at]).start()

        def plus(left, right):
            return tuple(tuple(a + b for a, b in zip(p, q)) for p, q in zip(left, right))

        def landed_copy(side, at):
            return pltpu.make_async_copy(off.at[side, at], off.at[side, at], brecv.at[side, at])

        def off_copy(side, at):
            return pltpu.make_async_copy(off.at[side, at], off_out.at[side, at], osem.at[side, at])

        def pair_copy(side, at):
            return pltpu.make_async_remote_copy(
                off.at[side, at],
                mates.at[side, at],
                psend.at[side, at],
                precv.at[side, at],
                device_id=(ta, 1, z),
                device_id_type=MESH,
            )

        def share_copy(side, at):
            return pltpu.make_async_remote_copy(
                carry_in.at[side, at],
                carry_in.at[side, at],
                csend.at[side, at],
                crecv.at[side, at],
                device_id=(ta, 0, z),
                device_id_type=MESH,
            )

        def chain_copy(side, at):
            return pltpu.make_async_remote_copy(
                sums.at[side, at],
                carry_in.at[side, at],
                ssend.at[side, at],
                crecv.at[side, at],
                device_id=(lax.rem(ta + 1, chips), 1, z),
                device_id_type=MESH,
            )

        mine = jnp.minimum(each, total - z * each) * 2

        def over(body):
            def step(t, carry):
                body(lax.rem(t, 2), t // 2)
                return carry

            lax.fori_loop(0, mine, step, 0)

        @pl.when(is_home & (me == 0))
        def _():
            def start(side, at):
                landed_copy(side, at).wait()
                pair_copy(side, at).start()
                off_copy(side, at).start()

            over(start)

            def rest(side, at):
                @pl.when(first)
                def _():
                    put(side, at, chunk(off, side, at))

                @pl.when(ta > 0)
                def _():
                    share_copy(side, at).wait_recv()
                    put(side, at, plus(chunk(off, side, at), moved(0, chunk(carry_in, side, at), side, at)))

            over(rest)

            def end(side, at):
                pair_copy(side, at).wait_send()

            over(end)

        @pl.when(is_home & (me == 1))
        def _():
            def step(side, at):
                landed_copy(side, at).wait()
                off_copy(side, at).start()
                pair_copy(side, at).wait_recv()
                both = plus(chunk(off, side, at), moved(0, chunk(mates, side, at), side, at))

                @pl.when(first)
                def _():
                    put(side, at, both)

                @pl.when(ta > 0)
                def _():
                    chain_copy(side, at).wait_recv()
                    share_copy(side, at).start()
                    put(side, at, plus(both, moved(1, chunk(carry_in, side, at), side, at)))

                @pl.when(passes_on)
                def _():
                    chain_copy(side, at).start()

            over(step)

            def end(side, at):
                @pl.when(ta > 0)
                def _():
                    share_copy(side, at).wait_send()

                @pl.when(passes_on)
                def _():
                    chain_copy(side, at).wait_send()

            over(end)

        @pl.when(is_home)
        def _():
            def end(side, at):
                off_copy(side, at).wait()
                pltpu.make_async_copy(sums.at[side, at], sum_out.at[side, at], usem.at[side, at]).wait()

            over(end)

        @pl.when(is_job)
        def _():
            def end(i, carry):
                @pl.when(jnp.logical_not(stays(i)))
                def _():
                    back_copy(i).wait_send()

                return carry

            lax.fori_loop(0, total, end, 0)

    ops = [factors, scan_factors, inv_even, inv_odd, fwd_even, fwd_odd, inv_x, inv_tw, fwd_x, fwd_tw]
    return pl.pallas_call(
        kernel,
        in_specs=[pl.BlockSpec(memory_space=pl.ANY)] * group
        + [pl.BlockSpec(memory_space=pltpu.VMEM)] * len(ops),
        out_specs=[pl.BlockSpec(memory_space=pl.ANY)] * 2,
        out_shape=[jax.ShapeDtypeStruct((2, each, 2, 3, 2, 8, 2 * low), jnp.float32)] * 2,
        scratch_shapes=[
            pltpu.VMEM((2, 3, 2, per, grid_size), jnp.float32),
            pltpu.VMEM((3, half, 2, 2, per, 4 * lanes), jnp.float32),
            pltpu.VMEM((3, half, 2, 2, kept, 5 * lanes), jnp.float32),
            pltpu.VMEM((2, 3, 2, kept, grid_size), jnp.float32),
            pltpu.VMEM((total, 2, 3, 2, 8, 2 * low), jnp.float32),
            *[pltpu.VMEM((2, each, 2, 3, 2, 8, 2 * low), jnp.float32)] * 4,
            pltpu.SemaphoreType.DMA((group,)),
            pltpu.SemaphoreType.DMA((2 * blocks,)),
            pltpu.SemaphoreType.DMA((2 * blocks,)),
            pltpu.SemaphoreType.DMA((half,)),
            pltpu.SemaphoreType.DMA((half,)),
            pltpu.SemaphoreType.DMA((total,)),
            *[pltpu.SemaphoreType.DMA((2, each))] * 9,
        ],
        compiler_params=pltpu.CompilerParams(
            collective_id=0, has_side_effects=True, vmem_limit_bytes=62 * 1024 * 1024
        ),
        name="fine_steps",
    )(*landed, *ops)


def finish(first, second, sums, off, zone, low):
    _, _, rows, grid_size = first.shape
    each = sums.shape[1]
    short = rows // 4
    limit = grid_size // 3

    def kernel(at_ref, first_ref, second_ref, sum_ref, off_ref, new_ref, res_ref, held):
        ky = lax.broadcasted_iota(jnp.int32, (rows, 1), 0) + at_ref[0] * rows
        inside = ky <= limit
        for base, extra, out in ((first_ref, sum_ref, new_ref), (second_ref, off_ref, res_ref)):
            for n in range(held.shape[0]):
                for side in range(2):
                    for h in range(2):
                        values = extra[side, :, h, 0, 0, :, n * 128 : (n + 1) * 128]
                        held[n, pl.ds(side + 2 * h, short, stride=4), :] = values.reshape(short, 128)
            for n in range(held.shape[0]):
                at = n * 128 if n * 128 < low else grid_size - 2 * low + n * 128
                lane = slice(at, at + 128)
                out[0, 0, 0, :, lane] = base[0, 0, :, lane] + jnp.where(inside, held[n], 0.0)
            if low * 2 < grid_size:
                lane = slice(low, grid_size - low)
                out[0, 0, 0, :, lane] = base[0, 0, :, lane]

    whole = pl.BlockSpec((1, 1, rows, grid_size), lambda f, c: (f, c, 0, 0))
    extra = pl.BlockSpec((2, each, 2, 1, 1, 8, 2 * low), lambda f, c: (0, 0, 0, f, c, 0, 0))
    out = pl.BlockSpec((1, 1, 1, rows, grid_size), lambda f, c: (0, f, c, 0, 0))
    return pl.pallas_call(
        kernel,
        grid=(3, 2),
        in_specs=[whole_smem(), whole, whole, extra, extra],
        out_specs=[out, out],
        out_shape=[jax.ShapeDtypeStruct((1, *first.shape), jnp.float32)] * 2,
        scratch_shapes=[pltpu.VMEM((2 * low // 128, rows, 128), jnp.float32)],
        name="finish",
    )(scalars(zone), first, second, sums, off)


def shards(c_state, init):
    rows, grid_size = c_state.shape[3:]
    group = lax.axis_size(SPACE)
    slabs = lax.axis_size(SLAB)
    slab = lax.axis_index(SLAB)
    core = lax.axis_index("core")
    zone = lax.axis_index(SPACE)
    short = rows // 4
    limit = grid_size // 3
    kept = -(-(limit // 4 + 1) // 8) * 8
    low = (limit // 128 + 1) * 128
    where = (group // 2 - 1, group // 2)

    def device(k, z):
        return k * group + z

    pieces = deal(c_state, init, slab == slabs - 1, zone, group)
    landed = []
    for n, piece in enumerate(pieces):
        links = [
            (device(k, (n + c * (group // 2)) % group), device(k // 2 * 2 + c, where[k % 2]))
            for k in range(slabs)
            for c in range(2)
        ]
        landed.append(lax.ppermute(piece, EVERY, links))
    links = [(device(k, z), device(k + 1, z)) for k in range(slabs - 1) for z in range(group)]
    before = jnp.where(slab == 0, init, lax.ppermute(c_state[0], EVERY, links))

    kx = waves_x(grid_size)
    tables = {
        "rows": row_tables(grid_size, kept),
        "inv_x": lane_tables(grid_size, 1.0),
        "fwd_x": lane_tables(grid_size, -1.0),
    }
    ky = 4 * jnp.arange(grid_size // 8, dtype=jnp.int32)[None] + 2 * jnp.arange(2, dtype=jnp.int32)[:, None]
    ky = (ky + core).astype(jnp.float32)[:, :, None]
    factors = jnp.stack(prop_factors(1.0, kx[None], ky, grid_size))

    ky = (zone * rows + jnp.arange(rows, dtype=jnp.int32)).astype(jnp.float32)[:, None]
    first = apply_array(init, prop_factors((CF * (slab + 1)).astype(jnp.float32), kx, ky, grid_size), kx, ky)
    second = apply_array(before, prop_factors(float(CF), kx, ky, grid_size), kx, ky) - c_state[0]
    kx_low = jnp.concatenate([kx[:, :low], kx[:, grid_size - low :]], axis=1)
    side, at, h, r = (
        jnp.arange(n, dtype=jnp.int32).reshape((-1,) + (1,) * (4 - k))
        for k, n in enumerate((2, short // 8, 2, 8))
    )
    ky = (4 * (zone * short + at * 8 + r) + 2 * h + side).astype(jnp.float32)
    scan_factors = jnp.stack(
        [jnp.stack(prop_factors(float(CF * n), kx_low, ky, grid_size)) for n in (1, 2)]
    )
    held = (landed, factors, scan_factors, tables, first, second)
    landed, factors, scan_factors, tables, first, second = lax.optimization_barrier(held)
    off, sums = fine_steps(landed, factors, scan_factors, tables, grid_size, kept, low, slabs, where)
    return tuple(finish(first, second, sums, off, zone, low))


def solution(mesh):
    slabs, space = mesh.devices.shape
    fine = Mesh(mesh.devices.reshape(slabs // 2, 2, space), EVERY)
    spec = P(SLAB, None, None, SPACE, None)
    return jax.shard_map(
        shards,
        mesh=fine,
        in_specs=(spec, P(None, None, SPACE, None)),
        out_specs=(spec, spec),
        check_vma=False,
    )
```

```python
import math

import jax
import jax.numpy as jnp
import numpy as np
from jax import lax
from jax.experimental import pallas as pl
from jax.experimental.pallas import tpu as pltpu
from jax.sharding import Mesh, PartitionSpec as P

CF = 2
CORIOLIS = 1.0
HYPERDIFFUSION = 0.25
COURANT = 0.4
RADIX = 8
ROWS = 32
SLAB = ("ta", "core")
SPACE = "sp"
EVERY = ("ta", "core", "sp")


def split_pair(values):
    high = values.astype(jnp.bfloat16)
    return high, (values - high.astype(jnp.float32)).astype(jnp.bfloat16)


def table_pair(values):
    high = lax.reduce_precision(values, 8, 7)
    return jnp.stack([high, values - high], axis=-3).astype(jnp.bfloat16)


def dot3(left, right):
    def one(a, b):
        return jnp.dot(a, b, preferred_element_type=jnp.float32)

    return one(left[0], right[0]) + (one(left[0], right[1]) + one(left[1], right[0]))


def small_fft(parts, sign):
    count = len(parts)
    if count == 1:
        return parts
    even = small_fft(parts[0::2], sign)
    odd = small_fft(parts[1::2], sign)
    low, high = [], []
    for k in range(count // 2):
        re, im = odd[k]
        if k == 0:
            tr, ti = re, im
        elif 4 * k == count:
            tr, ti = (-im, re) if sign > 0 else (im, -re)
        else:
            c = math.cos(2.0 * math.pi * k / count)
            s = sign * math.sin(2.0 * math.pi * k / count)
            tr, ti = re * c - im * s, re * s + im * c
        low.append((even[k][0] + tr, even[k][1] + ti))
        high.append((even[k][0] - tr, even[k][1] - ti))
    return low + high


def lane_tables(grid_size, sign):
    lanes = grid_size // RADIX
    n = np.arange(lanes)
    angle = 2.0 * np.pi * (n[:, None] * n[None, :] % lanes) / lanes
    c, s = np.cos(angle), sign * np.sin(angle)
    full = np.block([[c, s], [-s, c]]).astype(np.float32)
    high = full.astype(jnp.bfloat16)
    low = (full - high.astype(np.float32)).astype(jnp.bfloat16)
    turn = 2.0 * np.pi * (np.arange(RADIX)[:, None] * n[None, :]) / grid_size
    twiddle = np.stack([np.cos(turn), sign * np.sin(turn)]).astype(np.float32)
    return jnp.asarray(np.stack([high, low])), jnp.asarray(twiddle)


def prop_factors(steps, wave_x, wave_y, grid_size):
    time_step = COURANT / grid_size
    squared = wave_x * wave_x + wave_y * wave_y
    frequency = jnp.sqrt(CORIOLIS * CORIOLIS + squared)
    ratio = squared / (0.25 * grid_size * grid_size)
    log_damp = -HYPERDIFFUSION * (ratio * ratio) * (ratio * ratio)
    phase_angle = frequency * (steps * time_step)
    first_coef = jnp.sin(phase_angle) / frequency
    second_coef = (1.0 - jnp.cos(phase_angle)) / (frequency * frequency)
    damping = jnp.exp(steps * log_damp)
    return first_coef, second_coef, damping


def apply_parts(state, factors, kx, ky):
    first, second, damp = factors
    (xr, xi), (yr, yi), (hr, hi) = state
    done = []
    for x, y, p in ((xr, yr, -hi), (xi, yi, hr)):
        m1 = CORIOLIS * y - kx * p
        m2 = -CORIOLIS * x - ky * p
        m3 = kx * x + ky * y
        n1 = CORIOLIS * m2 - kx * m3
        n2 = -CORIOLIS * m1 - ky * m3
        n3 = kx * m1 + ky * m2
        done.append(
            (
                (x + first * m1 + second * n1) * damp,
                (y + first * m2 + second * n2) * damp,
                (p + first * m3 + second * n3) * damp,
            )
        )
    real, imag = done
    return ((real[0], imag[0]), (real[1], imag[1]), (imag[2], -real[2]))


def fine_steps(c_state, init, slabs, group, where):
    chips = slabs // 2
    MESH = pl.DeviceIdType.MESH
    rows, grid_size = c_state.shape[3:]
    short = rows // 4
    third = grid_size // 3
    kept = -(-(third // 4 + 1) // 8) * 8
    low = (third // 128 + 1) * 128
    per = grid_size // 8
    quarter = grid_size // 4
    lanes = grid_size // RADIX
    half = RADIX // 2
    blocks = per // ROWS
    limit = float(third)
    zones = -(-(third + 1) // rows)
    dt = COURANT / grid_size
    total = kept // 8
    each = short // 8
    inv_x, inv_tw = lane_tables(grid_size, 1.0)
    fwd_x, fwd_tw = lane_tables(grid_size, -1.0)

    def kernel(*refs):
        c_ref, i_ref, ix, itw, fx, ftw, off_out, sum_out, prev, wide_out = refs[:10]
        state, fields, modes, delta, off, mates, carry_in, sums = refs[10:18]
        fac, sfac, ie, io, fe, fo, held, dealt = refs[18:26]
        load, vsend, vrecv, gsend, grecv, wsem = refs[26:32]
        fsend, frecv, msend, mrecv, bsend, brecv, psend, precv, csend, crecv, ssend, srecv, osem, usem = refs[32:]
        ta, me, z = (lax.axis_index(name) for name in EVERY)
        mate = (ta, 1 - me, z)
        which = jnp.where(z == where[1], 1, 0)
        is_job = (z == where[0]) | (z == where[1])
        is_home = z < zones
        first = ta == 0
        shifts = (me == 1) & (ta < chips - 1)
        passes_on = shifts & is_home
        own_z = jnp.where(me == 1, where[1], where[0])
        own = 2 * ta + me
        home_is_own = is_job & is_home & (which == me)
        kx = lax.broadcasted_iota(jnp.int32, (1, grid_size), 1)
        kx = jnp.where(kx < grid_size // 2, kx, kx - grid_size).astype(jnp.float32)
        kx_low = jnp.concatenate([kx[:, :low], kx[:, grid_size - low :]], axis=1)
        slots = (2 * me, 2 - me)

        barrier = pltpu.get_barrier_semaphore()
        pl.semaphore_signal(barrier, inc=1, device_id=mate, device_id_type=MESH)
        for side in range(2):

            @pl.when(is_home & jnp.logical_not((z == own_z) & (me == side)))
            def _():
                pl.semaphore_signal(barrier, inc=1, device_id=(ta, side, own_z), device_id_type=MESH)

        for at in range(group):

            @pl.when(is_job & jnp.logical_not((z == at) & (me == which)))
            def _():
                pl.semaphore_signal(barrier, inc=1, device_id=(ta, which, at), device_id_type=MESH)

        @pl.when((me == 0) & (ta > 0))
        def _():
            pl.semaphore_signal(barrier, inc=1, device_id=(ta - 1, 1, z), device_id_type=MESH)

        @pl.when(is_home & (me == 1) & (ta > 0))
        def _():
            pl.semaphore_signal(barrier, inc=1, device_id=(ta - 1, 1, z), device_id_type=MESH)

        expected = (
            3
            + jnp.where(shifts, 1, 0)
            + jnp.where(passes_on, 1, 0)
            - jnp.where(z == own_z, 1, 0)
            + jnp.where(is_job, zones, 0)
            - jnp.where(home_is_own, 1, 0)
        )
        pl.semaphore_wait(barrier, expected)

        def prev_copy(n):
            f, c = n // 2, n % 2
            return pltpu.make_async_remote_copy(
                c_ref.at[0, f, c],
                prev.at[f, c],
                vsend.at[n],
                vrecv.at[n],
                device_id=(jnp.where(me == 1, lax.rem(ta + 1, chips), ta), 1 - me, z),
                device_id_type=MESH,
            )

        def state_part(n):
            return state.at[:, n // 2, n % 2, pl.ds(pl.multiple_of(z * short, 8), short)]

        def gather_copy(n, side):
            return pltpu.make_async_remote_copy(
                dealt.at[n, side],
                state_part(n),
                gsend.at[n, side],
                grecv.at[n, z],
                device_id=(ta, side, own_z),
                device_id_type=MESH,
            )

        def gather_wait(n, at):
            row = pl.ds(at * short, short)
            part = state.at[:, n // 2, n % 2, row]
            pltpu.make_async_copy(part, part, grecv.at[n, at]).wait()

        @pl.when((me == 0) | shifts)
        def _():
            for n in range(6):
                prev_copy(n).start()

        tiles = grid_size // 128

        def fetch(ref, n):
            copies = [
                pltpu.make_async_copy(
                    ref.at[n // 2, n % 2, :, pl.ds(at * 128, 128)], held.at[n % 2, at], load.at[n % 2, at]
                )
                for at in range(tiles)
            ]
            for copy in copies:
                copy.start()
            for copy in copies:
                copy.wait()

        def send_part(n):
            @pl.when(own == 0)
            def _():
                fetch(i_ref, n)

            @pl.when(own > 0)
            def _():
                pltpu.make_async_copy(prev.at[n // 2, n % 2], prev.at[n // 2, n % 2], vrecv.at[n]).wait()
                fetch(prev, n)

            for q in range(4):
                for at in range(tiles):
                    dealt[n, q % 2, q // 2, :, at * 128 : (at + 1) * 128] = held[
                        n % 2, at, pl.ds(q, short, stride=4), :
                    ]
            for side in range(2):
                here = (z == own_z) & (me == side)

                @pl.when(here)
                def _():
                    pltpu.make_async_copy(dealt.at[n, side], state_part(n), grecv.at[n, z]).start()

                @pl.when(jnp.logical_not(here))
                def _():
                    gather_copy(n, side).start()

        def waves(turns):
            angle = 2.0 * math.pi / grid_size * (turns & (grid_size - 1)).astype(jnp.float32)
            return jnp.cos(angle) / grid_size, jnp.sin(angle) / grid_size

        def put_pair(ref, lead, row, lane, values):
            for part, value in enumerate(split_pair(values)):
                ref[(*lead, part, row, lane)] = value

        def inverse_tables():
            for q in range(4):
                for at in range(0, quarter, 64):
                    y = lax.broadcasted_iota(jnp.int32, (64, per), 0) + at
                    ky = 4 * lax.broadcasted_iota(jnp.int32, (64, per), 1) + q
                    c, s = waves(y * ky)
                    weight = jnp.where(ky == 0, 1.0, 2.0)
                    c, s = c * weight, s * weight
                    row, next_row = slice(at, at + 64), slice(quarter + at, quarter + at + 64)
                    if q % 2 == 0:
                        put_pair(ie, (q // 2,), row, slice(0, per), c)
                        put_pair(ie, (q // 2,), row, slice(per, 2 * per), -s)
                    else:
                        base = (q // 2) * 2 * per
                        sign = 1.0 if q == 1 else -1.0
                        put_pair(io, (), row, slice(base, base + per), c)
                        put_pair(io, (), row, slice(base + per, base + 2 * per), -s)
                        put_pair(io, (), next_row, slice(base, base + per), sign * s)
                        put_pair(io, (), next_row, slice(base + per, base + 2 * per), sign * c)

        def forward_tables():
            for q in range(4):
                y = lax.broadcasted_iota(jnp.int32, (kept, quarter), 1)
                ky = 4 * lax.broadcasted_iota(jnp.int32, (kept, quarter), 0) + q
                c, s = waves(y * ky)
                if q % 2 == 0:
                    both = jnp.concatenate([c, -s], axis=0)
                    put_pair(fe, (q // 2,), slice(None), slice(None), both)
                else:
                    sign = 1.0 if q == 1 else -1.0
                    both = jnp.concatenate(
                        [
                            jnp.concatenate([c, -sign * s], axis=1),
                            jnp.concatenate([-s, -sign * c], axis=1),
                        ],
                        axis=0,
                    )
                    base = (q // 2) * 2 * kept
                    put_pair(fo, (), slice(base, base + 2 * kept), slice(None), both)

        def fine_factors(h):
            def body(b, carry):
                at = pl.multiple_of(b * 16, 16)
                made = prop_factors(1.0, kx, rows_ky(h, at, 16), grid_size)
                for n in range(3):
                    fac[n, h, pl.ds(at, 16)] = made[n]
                return carry

            lax.fori_loop(0, per // 16, body, 0)

        def scan_factors():
            def body(b, carry):
                at = b // 4
                side, h = b // 2 % 2, b % 2
                m = lax.broadcasted_iota(jnp.int32, (8, 1), 0) + (z * short + at * 8)
                ky = (4 * m + 2 * h + side).astype(jnp.float32)
                for k in range(2):
                    made = prop_factors(float(CF * (k + 1)), kx_low, ky, grid_size)
                    for n in range(3):
                        sfac[k, n, side, at, h] = made[n]
                return carry

            lax.fori_loop(0, 4 * each, body, 0)

        def wide_factors():
            def body(b, carry):
                at = pl.multiple_of(b * 8, 8)
                for part in range(2):
                    m = lax.broadcasted_iota(jnp.int32, (8, 1), 0) + (z * rows + part * (rows // 2) + at)
                    ky = m.astype(jnp.float32)
                    for k, steps in enumerate(((CF * (own + 1)).astype(jnp.float32), float(CF))):
                        made = prop_factors(steps, kx, ky, grid_size)
                        for n in range(3):
                            delta[k, n, part, pl.ds(at, 8)] = made[n]
                return carry

            lax.fori_loop(0, rows // 16, body, 0)
            wide_copy().start()

        def wide_copy():
            return pltpu.make_async_copy(delta.at[:, :, :, : rows // 2], wide_out, wsem)

        def back_part(i):
            return delta.at[:, :, :, pl.ds(pl.multiple_of(i * 8, 8), 8), : 2 * low]

        def back_copy(i):
            return pltpu.make_async_remote_copy(
                back_part(i),
                off.at[me, lax.rem(i, each)],
                bsend.at[i],
                brecv.at[me, lax.rem(i, each)],
                device_id=(ta, which, i // each),
                device_id_type=MESH,
            )

        def stays(i):
            return home_is_own & (i // each == z)

        def field_copy(f, h):
            lane = slice(f * lanes, (f + 1) * lanes)
            return pltpu.make_async_remote_copy(
                fields.at[2, :, h, :, :, lane],
                fields.at[me, :, h, :, :, lane],
                fsend.at[f, h],
                frecv.at[f, h],
                device_id=mate,
                device_id_type=MESH,
            )

        def mode_copy(j):
            return pltpu.make_async_remote_copy(
                modes.at[2, j],
                modes.at[me, j],
                msend.at[j],
                mrecv.at[j],
                device_id=mate,
                device_id_type=pl.DeviceIdType.MESH,
            )

        def rows_ky(h, at, count):
            m = lax.broadcasted_iota(jnp.int32, (count, 1), 0) + at
            return (4 * m + 2 * h + me).astype(jnp.float32)

        def inverse(f, h):
            def body(b, carry):
                at = pl.multiple_of(b * ROWS, ROWS)
                row = pl.ds(at, ROWS)
                if f < 3:
                    re, im = state[h, f, 0, row], state[h, f, 1, row]
                else:
                    ky = rows_ky(h, at, ROWS)
                    re = ky * state[h, 0, 1, row] - kx * state[h, 1, 1, row]
                    im = kx * state[h, 1, 0, row] - ky * state[h, 0, 0, row]
                parts = [
                    (re[:, n * lanes : (n + 1) * lanes], im[:, n * lanes : (n + 1) * lanes])
                    for n in range(RADIX)
                ]
                turned = []
                for k, (a, b_) in enumerate(small_fft(parts, 1.0)):
                    if k > 0:
                        c, s = itw[0, k : k + 1], itw[1, k : k + 1]
                        a, b_ = a * c - b_ * s, a * s + b_ * c
                    turned.append(jnp.concatenate([a, b_], axis=1))
                made = dot3(split_pair(jnp.concatenate(turned, axis=0)), (ix[0], ix[1]))
                for k in range(RADIX):
                    for c in range(2):
                        fields[slots[k // half], k % half, h, c, row, f * lanes : (f + 1) * lanes] = made[
                            k * ROWS : (k + 1) * ROWS, c * lanes : (c + 1) * lanes
                        ]
                return carry

            return body

        def middle(j, carry):
            def rows(c, h):
                return fields[c, j, h].reshape(2 * per, 4 * lanes)

            even = dot3((ie[0, 0], ie[0, 1]), split_pair(rows(0, 0)))
            other = dot3((ie[1, 0], ie[1, 1]), split_pair(rows(0, 1)))
            odd = dot3(
                (io[0], io[1]), split_pair(jnp.concatenate([rows(1, 0), rows(1, 1)], axis=0))
            )
            re, im = odd[: 2 * per], odd[2 * per :]
            plus, minus = even + other, even - other
            made = []
            for grid in (plus + re, minus - im, plus - re, minus + im):
                u, v, h, w = (grid[:, f * lanes : (f + 1) * lanes] for f in range(4))
                made.append(
                    jnp.concatenate([w * v, w * u, 0.5 * (u * u + v * v), h * u, h * v], axis=1)
                )
            a, b = made[0] + made[2], made[1] + made[3]
            for h, term in enumerate((a + b, a - b)):
                got = dot3((fe[h, 0], fe[h, 1]), split_pair(term))
                modes[slots[0], j, h] = got.reshape(2, kept, 5 * lanes)
            term = jnp.concatenate([made[0] - made[2], made[1] - made[3]], axis=0)
            got = dot3((fo[0], fo[1]), split_pair(term))
            for h in range(2):
                modes[slots[1], j, h] = got[2 * kept * h : 2 * kept * (h + 1)].reshape(
                    2, kept, 5 * lanes
                )
            mode_copy(j).start()
            return carry

        def read(ref, at):
            return tuple(
                tuple(
                    jnp.concatenate([ref[h, f, c, pl.ds(at, 8)] for h in range(2)], axis=0)
                    for c in range(2)
                )
                for f in range(3)
            )

        def write(ref, at, values):
            for f in range(3):
                for c in range(2):
                    for h in range(2):
                        ref[h, f, c, pl.ds(at, 8)] = values[f][c][8 * h : 8 * h + 8]

        def rows_of(i):
            at = pl.multiple_of(i * 8, 8)
            ky = jnp.concatenate([rows_ky(h, at, 8) for h in range(2)], axis=0)
            factors = tuple(
                jnp.concatenate([fac[n, h, pl.ds(at, 8)] for h in range(2)], axis=0) for n in range(3)
            )
            return at, ky, factors

        def plain(i, carry):
            at, ky, factors = rows_of(i)
            write(state, at, apply_parts(read(state, at), factors, kx, ky))
            return carry

        def turn_of(n):
            last = total - (zones - 1) * each
            m = n - last * zones
            others = max(zones - 1, 1)
            early = lax.rem(n, zones) * each + n // zones
            late = lax.rem(m + others, others) * each + last + m // others
            return jnp.where(m < 0, early, late)

        def forward(step):
            def body(n, carry):
                i = n if step == 0 else turn_of(n)
                at, ky, factors = rows_of(i)

                def piece(f, c, k):
                    return jnp.concatenate(
                        [
                            modes[k // half, k % half, h, c, pl.ds(at, 8), f * lanes : (f + 1) * lanes]
                            for h in range(2)
                        ],
                        axis=0,
                    )

                stacked = jnp.concatenate(
                    [
                        jnp.concatenate([piece(f, 0, k), piece(f, 1, k)], axis=1)
                        for f in range(5)
                        for k in range(RADIX)
                    ],
                    axis=0,
                )
                made = dot3(split_pair(stacked), (fx[0], fx[1]))
                found = []
                for f in range(5):
                    parts = []
                    for k in range(RADIX):
                        start = (f * RADIX + k) * 16
                        a = made[start : start + 16, :lanes]
                        b = made[start : start + 16, lanes:]
                        if k > 0:
                            c, s = ftw[0, k : k + 1], ftw[1, k : k + 1]
                            a, b = a * c - b * s, a * s + b * c
                        parts.append((a, b))
                    parts = small_fft(parts, -1.0)
                    found.append(
                        tuple(jnp.concatenate([p[c] for p in parts], axis=1) for c in range(2))
                    )
                (ar, ai), (br, bi), (kr, ki), (pr, pi), (qr, qi) = found
                inside = (jnp.abs(kx) <= limit) & (ky <= limit)

                def keep(values):
                    return jnp.where(inside, dt * values, 0.0)

                change = (
                    (keep(ar + kx * ki), keep(ai - kx * kr)),
                    (keep(ky * ki - br), -keep(bi + ky * kr)),
                    (keep(kx * pi + ky * qi), -keep(kx * pr + ky * qr)),
                )

                def add(left, right):
                    return tuple(tuple(a + b for a, b in zip(p, q)) for p, q in zip(left, right))

                if step == 0:
                    change = apply_parts(change, factors, kx, ky)
                    write(delta, at, change)
                    moved = apply_parts(read(state, at), factors, kx, ky)
                    write(state, at, add(moved, change))
                else:
                    change = add(change, read(delta, at))
                    change = apply_parts(change, factors, kx, ky)
                    for f in range(3):
                        for c in range(2):
                            for h in range(2):
                                value = change[f][c][8 * h : 8 * h + 8]
                                delta[h, f, c, pl.ds(at, 8), :low] = value[:, :low]
                                delta[h, f, c, pl.ds(at, 8), low : 2 * low] = value[:, grid_size - low :]

                    @pl.when(stays(i))
                    def _():
                        to = lax.rem(i, each)
                        pltpu.make_async_copy(back_part(i), off.at[me, to], brecv.at[me, to]).start()

                    @pl.when(is_job & jnp.logical_not(stays(i)))
                    def _():
                        back_copy(i).start()

                return carry

            return body

        fillers = (
            inverse_tables,
            forward_tables,
            lambda: fine_factors(0),
            lambda: fine_factors(1),
            scan_factors,
            wide_factors,
        )
        for n in range(6):
            send_part(n)
            fillers[n]()

        def steps():
            for step in range(CF):
                for f in (0, 1, 3, 2):
                    if step == 0 and f < 3:
                        for n in (2 * f, 2 * f + 1):
                            for at in range(group):
                                gather_wait(n, at)
                    for h in range(2):
                        lax.fori_loop(0, blocks, inverse(f, h), 0)
                        field_copy(f, h).start()
                if step == 0:
                    wide_copy().wait()
                for f in range(4):
                    for h in range(2):
                        field_copy(f, h).wait()
                lax.fori_loop(0, half, middle, 0)
                if step < CF - 1:
                    lax.fori_loop(kept // 8, per // 8, plain, 0)
                for j in range(half):
                    mode_copy(j).wait()
                lax.fori_loop(0, kept // 8, forward(step), 0)

        pl.when(is_job)(steps)

        @pl.when(jnp.logical_not(is_job))
        def _():
            wide_copy().wait()

        def chunk(ref, side, at):
            return tuple(
                tuple(jnp.concatenate([ref[side, at, h, f, c] for h in range(2)], axis=0) for c in range(2))
                for f in range(3)
            )

        def moved(n, values, side, at):
            m = lax.broadcasted_iota(jnp.int32, (8, 1), 0) + (z * short + at * 8)
            ky = jnp.concatenate([4 * m + 2 * h + side for h in range(2)], axis=0).astype(jnp.float32)
            factors = tuple(
                jnp.concatenate([sfac[n, k, side, at, h] for h in range(2)], axis=0) for k in range(3)
            )
            return apply_parts(values, factors, kx_low, ky)

        def put(side, at, values):
            for f in range(3):
                for c in range(2):
                    for h in range(2):
                        sums[side, at, h, f, c] = values[f][c][8 * h : 8 * h + 8]
            pltpu.make_async_copy(sums.at[side, at], sum_out.at[side, at], usem.at[side, at]).start()

        def plus(left, right):
            return tuple(tuple(a + b for a, b in zip(p, q)) for p, q in zip(left, right))

        def landed_copy(side, at):
            return pltpu.make_async_copy(off.at[side, at], off.at[side, at], brecv.at[side, at])

        def off_copy(side, at):
            return pltpu.make_async_copy(off.at[side, at], off_out.at[side, at], osem.at[side, at])

        def pair_copy(side, at):
            return pltpu.make_async_remote_copy(
                off.at[side, at],
                mates.at[side, at],
                psend.at[side, at],
                precv.at[side, at],
                device_id=(ta, 1, z),
                device_id_type=MESH,
            )

        def share_copy(side, at):
            return pltpu.make_async_remote_copy(
                carry_in.at[side, at],
                carry_in.at[side, at],
                csend.at[side, at],
                crecv.at[side, at],
                device_id=(ta, 0, z),
                device_id_type=MESH,
            )

        def chain_copy(side, at):
            return pltpu.make_async_remote_copy(
                sums.at[side, at],
                carry_in.at[side, at],
                ssend.at[side, at],
                crecv.at[side, at],
                device_id=(lax.rem(ta + 1, chips), 1, z),
                device_id_type=MESH,
            )

        mine = jnp.minimum(each, total - z * each) * 2

        def over(body):
            def step(t, carry):
                body(lax.rem(t, 2), t // 2)
                return carry

            lax.fori_loop(0, mine, step, 0)

        @pl.when(is_home & (me == 0))
        def _():
            def start(side, at):
                landed_copy(side, at).wait()
                pair_copy(side, at).start()
                off_copy(side, at).start()

            over(start)

            def rest(side, at):
                @pl.when(first)
                def _():
                    put(side, at, chunk(off, side, at))

                @pl.when(ta > 0)
                def _():
                    share_copy(side, at).wait_recv()
                    put(side, at, plus(chunk(off, side, at), moved(0, chunk(carry_in, side, at), side, at)))

            over(rest)

            def end(side, at):
                pair_copy(side, at).wait_send()

            over(end)

        @pl.when(is_home & (me == 1))
        def _():
            def step(side, at):
                landed_copy(side, at).wait()
                off_copy(side, at).start()
                pair_copy(side, at).wait_recv()
                both = plus(chunk(off, side, at), moved(0, chunk(mates, side, at), side, at))

                @pl.when(first)
                def _():
                    put(side, at, both)

                @pl.when(ta > 0)
                def _():
                    chain_copy(side, at).wait_recv()
                    share_copy(side, at).start()
                    put(side, at, plus(both, moved(1, chunk(carry_in, side, at), side, at)))

                @pl.when(passes_on)
                def _():
                    chain_copy(side, at).start()

            over(step)

            def end(side, at):
                @pl.when(ta > 0)
                def _():
                    share_copy(side, at).wait_send()

                @pl.when(passes_on)
                def _():
                    chain_copy(side, at).wait_send()

            over(end)

        @pl.when(is_home)
        def _():
            def end(side, at):
                off_copy(side, at).wait()
                pltpu.make_async_copy(sums.at[side, at], sum_out.at[side, at], usem.at[side, at]).wait()

            over(end)

        @pl.when((me == 0) | shifts)
        def _():
            for n in range(6):
                prev_copy(n).wait_send()

        for n in range(6):
            for side in range(2):

                @pl.when(jnp.logical_not((z == own_z) & (me == side)))
                def _():
                    gather_copy(n, side).wait_send()

        @pl.when(is_job)
        def _():
            def end(i, carry):
                @pl.when(jnp.logical_not(stays(i)))
                def _():
                    back_copy(i).wait_send()

                return carry

            lax.fori_loop(0, total, end, 0)

    return pl.pallas_call(
        kernel,
        in_specs=[pl.BlockSpec(memory_space=pl.ANY)] * 2 + [pl.BlockSpec(memory_space=pltpu.VMEM)] * 4,
        out_specs=[pl.BlockSpec(memory_space=pl.ANY)] * 4,
        out_shape=[jax.ShapeDtypeStruct((2, each, 2, 3, 2, 8, 2 * low), jnp.float32)] * 2
        + [
            jax.ShapeDtypeStruct((3, 2, rows, grid_size), jnp.float32),
            jax.ShapeDtypeStruct((2, 3, 2, rows // 2, grid_size), jnp.float32),
        ],
        scratch_shapes=[
            pltpu.VMEM((2, 3, 2, per, grid_size), jnp.float32),
            pltpu.VMEM((3, half, 2, 2, per, 4 * lanes), jnp.float32),
            pltpu.VMEM((3, half, 2, 2, kept, 5 * lanes), jnp.float32),
            pltpu.VMEM((2, 3, 2, kept, grid_size), jnp.float32),
            *[pltpu.VMEM((2, each, 2, 3, 2, 8, 2 * low), jnp.float32)] * 4,
            pltpu.VMEM((3, 2, per, grid_size), jnp.float32),
            pltpu.VMEM((2, 3, 2, each, 2, 8, 2 * low), jnp.float32),
            pltpu.VMEM((2, 2, quarter, quarter), jnp.bfloat16),
            pltpu.VMEM((2, 2 * quarter, 2 * quarter), jnp.bfloat16),
            pltpu.VMEM((2, 2, 2 * kept, quarter), jnp.bfloat16),
            pltpu.VMEM((2, 4 * kept, 2 * quarter), jnp.bfloat16),
            pltpu.VMEM((2, grid_size // 128, rows, 128), jnp.float32),
            pltpu.VMEM((6, 2, 2, short, grid_size), jnp.float32),
            pltpu.SemaphoreType.DMA((2, grid_size // 128)),
            pltpu.SemaphoreType.DMA((6,)),
            pltpu.SemaphoreType.DMA((6,)),
            pltpu.SemaphoreType.DMA((6, 2)),
            pltpu.SemaphoreType.DMA((6, group)),
            pltpu.SemaphoreType.DMA,
            pltpu.SemaphoreType.DMA((4, 2)),
            pltpu.SemaphoreType.DMA((4, 2)),
            pltpu.SemaphoreType.DMA((half,)),
            pltpu.SemaphoreType.DMA((half,)),
            pltpu.SemaphoreType.DMA((total,)),
            *[pltpu.SemaphoreType.DMA((2, each))] * 9,
        ],
        compiler_params=pltpu.CompilerParams(
            collective_id=0, has_side_effects=True, vmem_limit_bytes=63 * 1024 * 1024
        ),
        name="fine_steps",
    )(c_state, init, inv_x, inv_tw, fwd_x, fwd_tw)


def scalars(*values):
    return jnp.stack([jnp.asarray(v, jnp.int32) for v in values])


def finish(c_state, init, prev, wide, sums, off, slab, zone):
    rows, grid_size = c_state.shape[3:]
    each, low = sums.shape[1], sums.shape[-1] // 2
    limit = grid_size // 3
    step = rows // each

    def kernel(at_ref, c_ref, i_ref, p_ref, w_ref, sum_ref, off_ref, new_ref, res_ref, held):
        kx = lax.broadcasted_iota(jnp.int32, (1, grid_size), 1)
        kx = jnp.where(kx < grid_size // 2, kx, kx - grid_size).astype(jnp.float32)
        row = lax.broadcasted_iota(jnp.int32, (step, 1), 0) + at_ref[1] * rows + pl.program_id(0) * step
        ky = row.astype(jnp.float32)
        inside = row <= limit

        def moved(fields, k):
            return apply_parts(fields, (w_ref[k, 0], w_ref[k, 1], w_ref[k, 2]), kx, ky)

        def placed(ref, f, c):
            for n in range(held.shape[0]):
                for side in range(2):
                    for h in range(2):
                        held[n, pl.ds(side + 2 * h, 8, stride=4), :] = ref[
                            side, 0, h, f, c, :, n * 128 : (n + 1) * 128
                        ]
            found = [jnp.where(inside, held[n], 0.0) for n in range(held.shape[0])]
            count = low // 128
            between = [jnp.zeros((step, grid_size - 2 * low), jnp.float32)] if 2 * low < grid_size else []
            return jnp.concatenate(found[:count] + between + found[count:], axis=1)

        is_first = at_ref[0] == 0
        start = tuple(tuple(i_ref[f, c] for c in range(2)) for f in range(3))
        before = tuple(tuple(jnp.where(is_first, i_ref[f, c], p_ref[f, c]) for c in range(2)) for f in range(3))
        new, end = moved(start, 0), moved(before, 1)
        for f in range(3):
            for c in range(2):
                new_ref[0, f, c] = new[f][c] + placed(sum_ref, f, c)
                res_ref[0, f, c] = (end[f][c] + placed(off_ref, f, c)) - c_ref[0, f, c]

    whole = pl.BlockSpec((1, 3, 2, step, grid_size), lambda i: (0, 0, 0, i, 0))
    part = pl.BlockSpec((3, 2, step, grid_size), lambda i: (0, 0, i, 0))
    factor = pl.BlockSpec((2, 3, step, grid_size), lambda i: (0, 0, i, 0))
    extra = pl.BlockSpec((2, 1, 2, 3, 2, 8, 2 * low), lambda i: (0, i, 0, 0, 0, 0, 0))
    return pl.pallas_call(
        kernel,
        grid=(each,),
        in_specs=[pl.BlockSpec(memory_space=pltpu.SMEM), whole, part, part, factor, extra, extra],
        out_specs=[whole, whole],
        out_shape=[jax.ShapeDtypeStruct(c_state.shape, jnp.float32)] * 2,
        scratch_shapes=[pltpu.VMEM((2 * low // 128, step, 128), jnp.float32)],
        name="finish",
    )(scalars(slab, zone), c_state, init, prev, wide, sums, off)


def shards(c_state, init):
    rows, grid_size = c_state.shape[3:]
    group = lax.axis_size(SPACE)
    slabs = lax.axis_size(SLAB)
    where = (group // 2 - 1, group // 2)
    off, sums, prev, wide = fine_steps(c_state, init, slabs, group, where)
    wide = wide.reshape(2, 3, rows, grid_size)
    return tuple(
        finish(c_state, init, prev, wide, sums, off, lax.axis_index(SLAB), lax.axis_index(SPACE))
    )


def solution(mesh):
    slabs, space = mesh.devices.shape
    fine = Mesh(mesh.devices.reshape(slabs // 2, 2, space), EVERY)
    spec = P(SLAB, None, None, SPACE, None)
    return jax.shard_map(
        shards,
        mesh=fine,
        in_specs=(spec, P(None, None, SPACE, None)),
        out_specs=(spec, spec),
        check_vma=False,
    )
```

```python
import math

import jax
import jax.numpy as jnp
import numpy as np
from jax import lax
from jax.experimental import pallas as pl
from jax.experimental.pallas import tpu as pltpu
from jax.sharding import Mesh, PartitionSpec as P

CF = 2
CORIOLIS = 1.0
HYPERDIFFUSION = 0.25
COURANT = 0.4
RADIX = 8
ROWS = 32
SLAB = ("ta", "core")
SPACE = "sp"
EVERY = ("ta", "core", "sp")


def split_pair(values):
    high = values.astype(jnp.bfloat16)
    return high, (values - high.astype(jnp.float32)).astype(jnp.bfloat16)


def table_pair(values):
    high = lax.reduce_precision(values, 8, 7)
    return jnp.stack([high, values - high], axis=-3).astype(jnp.bfloat16)


def dot3(left, right):
    def one(a, b):
        return jnp.dot(a, b, preferred_element_type=jnp.float32)

    return one(left[0], right[0]) + (one(left[0], right[1]) + one(left[1], right[0]))


def small_fft(parts, sign):
    count = len(parts)
    if count == 1:
        return parts
    even = small_fft(parts[0::2], sign)
    odd = small_fft(parts[1::2], sign)
    low, high = [], []
    for k in range(count // 2):
        re, im = odd[k]
        if k == 0:
            tr, ti = re, im
        elif 4 * k == count:
            tr, ti = (-im, re) if sign > 0 else (im, -re)
        else:
            c = math.cos(2.0 * math.pi * k / count)
            s = sign * math.sin(2.0 * math.pi * k / count)
            tr, ti = re * c - im * s, re * s + im * c
        low.append((even[k][0] + tr, even[k][1] + ti))
        high.append((even[k][0] - tr, even[k][1] - ti))
    return low + high


def lane_tables(grid_size, sign):
    lanes = grid_size // RADIX
    n = np.arange(lanes)
    angle = 2.0 * np.pi * (n[:, None] * n[None, :] % lanes) / lanes
    c, s = np.cos(angle), sign * np.sin(angle)
    full = np.block([[c, s], [-s, c]]).astype(np.float32)
    high = full.astype(jnp.bfloat16)
    low = (full - high.astype(np.float32)).astype(jnp.bfloat16)
    turn = 2.0 * np.pi * (np.arange(RADIX)[:, None] * n[None, :]) / grid_size
    twiddle = np.stack([np.cos(turn), sign * np.sin(turn)]).astype(np.float32)
    return jnp.asarray(np.stack([high, low])), jnp.asarray(twiddle)


def prop_factors(steps, wave_x, wave_y, grid_size):
    time_step = COURANT / grid_size
    squared = wave_x * wave_x + wave_y * wave_y
    frequency = jnp.sqrt(CORIOLIS * CORIOLIS + squared)
    ratio = squared / (0.25 * grid_size * grid_size)
    log_damp = -HYPERDIFFUSION * (ratio * ratio) * (ratio * ratio)
    phase_angle = frequency * (steps * time_step)
    first_coef = jnp.sin(phase_angle) / frequency
    second_coef = (1.0 - jnp.cos(phase_angle)) / (frequency * frequency)
    damping = jnp.exp(steps * log_damp)
    return first_coef, second_coef, damping


def apply_parts(state, factors, kx, ky):
    first, second, damp = factors
    (xr, xi), (yr, yi), (hr, hi) = state
    done = []
    for x, y, p in ((xr, yr, -hi), (xi, yi, hr)):
        m1 = CORIOLIS * y - kx * p
        m2 = -CORIOLIS * x - ky * p
        m3 = kx * x + ky * y
        n1 = CORIOLIS * m2 - kx * m3
        n2 = -CORIOLIS * m1 - ky * m3
        n3 = kx * m1 + ky * m2
        done.append(
            (
                (x + first * m1 + second * n1) * damp,
                (y + first * m2 + second * n2) * damp,
                (p + first * m3 + second * n3) * damp,
            )
        )
    real, imag = done
    return ((real[0], imag[0]), (real[1], imag[1]), (imag[2], -real[2]))


def fine_steps(c_state, init, slabs, group, where):
    chips = slabs // 2
    MESH = pl.DeviceIdType.MESH
    rows, grid_size = c_state.shape[3:]
    short = rows // 4
    third = grid_size // 3
    kept = -(-(third // 4 + 1) // 8) * 8
    low = (third // 128 + 1) * 128
    per = grid_size // 8
    quarter = grid_size // 4
    lanes = grid_size // RADIX
    half = RADIX // 2
    blocks = per // ROWS
    limit = float(third)
    zones = -(-(third + 1) // rows)
    dt = COURANT / grid_size
    total = kept // 8
    each = short // 8
    inv_x, inv_tw = lane_tables(grid_size, 1.0)
    fwd_x, fwd_tw = lane_tables(grid_size, -1.0)

    def kernel(*refs):
        c_ref, i_ref, ix, itw, fx, ftw, new_out, res_out, prev = refs[:9]
        state, fields, modes, delta, off, mates, carry_in, sums = refs[9:17]
        fac, sfac, ie, io, fe, fo, held, dealt = refs[17:25]
        load, vsend, vrecv, gsend, grecv, bases = refs[25:31]
        fsend, frecv, msend, mrecv, bsend, brecv, psend, precv, csend, crecv, ssend, osem = refs[31:]
        ta, me, z = (lax.axis_index(name) for name in EVERY)
        mate = (ta, 1 - me, z)
        which = jnp.where(z == where[1], 1, 0)
        is_job = (z == where[0]) | (z == where[1])
        is_home = z < zones
        first = ta == 0
        shifts = (me == 1) & (ta < chips - 1)
        passes_on = shifts & is_home
        own_z = jnp.where(me == 1, where[1], where[0])
        own = 2 * ta + me
        home_is_own = is_job & is_home & (which == me)
        kx = lax.broadcasted_iota(jnp.int32, (1, grid_size), 1)
        kx = jnp.where(kx < grid_size // 2, kx, kx - grid_size).astype(jnp.float32)
        kx_low = jnp.concatenate([kx[:, :low], kx[:, grid_size - low :]], axis=1)
        slots = (2 * me, 2 - me)

        barrier = pltpu.get_barrier_semaphore()
        pl.semaphore_signal(barrier, inc=1, device_id=mate, device_id_type=MESH)
        for side in range(2):

            @pl.when(is_home & jnp.logical_not((z == own_z) & (me == side)))
            def _():
                pl.semaphore_signal(barrier, inc=1, device_id=(ta, side, own_z), device_id_type=MESH)

        for at in range(group):

            @pl.when(is_job & jnp.logical_not((z == at) & (me == which)))
            def _():
                pl.semaphore_signal(barrier, inc=1, device_id=(ta, which, at), device_id_type=MESH)

        @pl.when((me == 0) & (ta > 0))
        def _():
            pl.semaphore_signal(barrier, inc=1, device_id=(ta - 1, 1, z), device_id_type=MESH)

        @pl.when(is_home & (me == 1) & (ta > 0))
        def _():
            pl.semaphore_signal(barrier, inc=1, device_id=(ta - 1, 1, z), device_id_type=MESH)

        expected = (
            3
            + jnp.where(shifts, 1, 0)
            + jnp.where(passes_on, 1, 0)
            - jnp.where(z == own_z, 1, 0)
            + jnp.where(is_job, zones, 0)
            - jnp.where(home_is_own, 1, 0)
        )
        pl.semaphore_wait(barrier, expected)

        def prev_copy(n):
            f, c = n // 2, n % 2
            return pltpu.make_async_remote_copy(
                c_ref.at[0, f, c],
                prev.at[f, c],
                vsend.at[n],
                vrecv.at[n],
                device_id=(jnp.where(me == 1, lax.rem(ta + 1, chips), ta), 1 - me, z),
                device_id_type=MESH,
            )

        def state_part(n):
            return state.at[:, n // 2, n % 2, pl.ds(pl.multiple_of(z * short, 8), short)]

        def gather_copy(n, side):
            return pltpu.make_async_remote_copy(
                dealt.at[n, side],
                state_part(n),
                gsend.at[n, side],
                grecv.at[n, z],
                device_id=(ta, side, own_z),
                device_id_type=MESH,
            )

        def gather_wait(n, at):
            row = pl.ds(at * short, short)
            part = state.at[:, n // 2, n % 2, row]
            pltpu.make_async_copy(part, part, grecv.at[n, at]).wait()

        @pl.when((me == 0) | shifts)
        def _():
            for n in range(6):
                prev_copy(n).start()

        tiles = grid_size // 128

        def fetch(ref, n):
            copies = [
                pltpu.make_async_copy(
                    ref.at[n // 2, n % 2, :, pl.ds(at * 128, 128)], held.at[n % 2, at], load.at[n % 2, at]
                )
                for at in range(tiles)
            ]
            for copy in copies:
                copy.start()
            for copy in copies:
                copy.wait()

        def send_part(n):
            @pl.when(own == 0)
            def _():
                fetch(i_ref, n)

            @pl.when(own > 0)
            def _():
                pltpu.make_async_copy(prev.at[n // 2, n % 2], prev.at[n // 2, n % 2], vrecv.at[n]).wait()
                fetch(prev, n)

            for q in range(4):
                for at in range(tiles):
                    dealt[n, q % 2, q // 2, :, at * 128 : (at + 1) * 128] = held[
                        n % 2, at, pl.ds(q, short, stride=4), :
                    ]
            for side in range(2):
                here = (z == own_z) & (me == side)

                @pl.when(here)
                def _():
                    pltpu.make_async_copy(dealt.at[n, side], state_part(n), grecv.at[n, z]).start()

                @pl.when(jnp.logical_not(here))
                def _():
                    gather_copy(n, side).start()

        def waves(turns):
            angle = 2.0 * math.pi / grid_size * (turns & (grid_size - 1)).astype(jnp.float32)
            return jnp.cos(angle) / grid_size, jnp.sin(angle) / grid_size

        def put_pair(ref, lead, row, lane, values):
            for part, value in enumerate(split_pair(values)):
                ref[(*lead, part, row, lane)] = value

        def inverse_tables():
            for q in range(4):
                for at in range(0, quarter, 64):
                    y = lax.broadcasted_iota(jnp.int32, (64, per), 0) + at
                    ky = 4 * lax.broadcasted_iota(jnp.int32, (64, per), 1) + q
                    c, s = waves(y * ky)
                    weight = jnp.where(ky == 0, 1.0, 2.0)
                    c, s = c * weight, s * weight
                    row, next_row = slice(at, at + 64), slice(quarter + at, quarter + at + 64)
                    if q % 2 == 0:
                        put_pair(ie, (q // 2,), row, slice(0, per), c)
                        put_pair(ie, (q // 2,), row, slice(per, 2 * per), -s)
                    else:
                        base = (q // 2) * 2 * per
                        sign = 1.0 if q == 1 else -1.0
                        put_pair(io, (), row, slice(base, base + per), c)
                        put_pair(io, (), row, slice(base + per, base + 2 * per), -s)
                        put_pair(io, (), next_row, slice(base, base + per), sign * s)
                        put_pair(io, (), next_row, slice(base + per, base + 2 * per), sign * c)

        def forward_tables():
            for q in range(4):
                y = lax.broadcasted_iota(jnp.int32, (kept, quarter), 1)
                ky = 4 * lax.broadcasted_iota(jnp.int32, (kept, quarter), 0) + q
                c, s = waves(y * ky)
                if q % 2 == 0:
                    both = jnp.concatenate([c, -s], axis=0)
                    put_pair(fe, (q // 2,), slice(None), slice(None), both)
                else:
                    sign = 1.0 if q == 1 else -1.0
                    both = jnp.concatenate(
                        [
                            jnp.concatenate([c, -sign * s], axis=1),
                            jnp.concatenate([-s, -sign * c], axis=1),
                        ],
                        axis=0,
                    )
                    base = (q // 2) * 2 * kept
                    put_pair(fo, (), slice(base, base + 2 * kept), slice(None), both)

        def fine_factors(h):
            def body(b, carry):
                at = pl.multiple_of(b * 16, 16)
                made = prop_factors(1.0, kx, rows_ky(h, at, 16), grid_size)
                for n in range(3):
                    fac[n, h, pl.ds(at, 16)] = made[n]
                return carry

            lax.fori_loop(0, per // 16, body, 0)

        def scan_factors():
            def body(b, carry):
                at = b // 4
                side, h = b // 2 % 2, b % 2
                m = lax.broadcasted_iota(jnp.int32, (8, 1), 0) + (z * short + at * 8)
                ky = (4 * m + 2 * h + side).astype(jnp.float32)
                for k in range(2):
                    made = prop_factors(float(CF * (k + 1)), kx_low, ky, grid_size)
                    for n in range(3):
                        sfac[k, n, side, at, h] = made[n]
                return carry

            lax.fori_loop(0, 4 * each, body, 0)

        def back_part(i, h):
            return delta.at[h, :, :, pl.ds(pl.multiple_of(i * 8, 8), 8), : 2 * low]

        def back_copy(i, h):
            return pltpu.make_async_remote_copy(
                back_part(i, h),
                off.at[me, lax.rem(i, each), h],
                bsend.at[i, h],
                brecv.at[me, lax.rem(i, each), h],
                device_id=(ta, which, i // each),
                device_id_type=MESH,
            )

        def stays(i):
            return home_is_own & (i // each == z)

        def field_copy(f, h):
            lane = slice(f * lanes, (f + 1) * lanes)
            return pltpu.make_async_remote_copy(
                fields.at[2, :, h, :, :, lane],
                fields.at[me, :, h, :, :, lane],
                fsend.at[f, h],
                frecv.at[f, h],
                device_id=mate,
                device_id_type=MESH,
            )

        def mode_copy(j):
            return pltpu.make_async_remote_copy(
                modes.at[2, j],
                modes.at[me, j],
                msend.at[j],
                mrecv.at[j],
                device_id=mate,
                device_id_type=pl.DeviceIdType.MESH,
            )

        def rows_ky(h, at, count):
            m = lax.broadcasted_iota(jnp.int32, (count, 1), 0) + at
            return (4 * m + 2 * h + me).astype(jnp.float32)

        def inverse(f, h):
            def body(b, carry):
                at = pl.multiple_of(b * ROWS, ROWS)
                row = pl.ds(at, ROWS)
                if f < 3:
                    re, im = state[h, f, 0, row], state[h, f, 1, row]
                else:
                    ky = rows_ky(h, at, ROWS)
                    re = ky * state[h, 0, 1, row] - kx * state[h, 1, 1, row]
                    im = kx * state[h, 1, 0, row] - ky * state[h, 0, 0, row]
                parts = [
                    (re[:, n * lanes : (n + 1) * lanes], im[:, n * lanes : (n + 1) * lanes])
                    for n in range(RADIX)
                ]
                turned = []
                for k, (a, b_) in enumerate(small_fft(parts, 1.0)):
                    if k > 0:
                        c, s = itw[0, k : k + 1], itw[1, k : k + 1]
                        a, b_ = a * c - b_ * s, a * s + b_ * c
                    turned.append(jnp.concatenate([a, b_], axis=1))
                made = dot3(split_pair(jnp.concatenate(turned, axis=0)), (ix[0], ix[1]))
                for k in range(RADIX):
                    for c in range(2):
                        fields[slots[k // half], k % half, h, c, row, f * lanes : (f + 1) * lanes] = made[
                            k * ROWS : (k + 1) * ROWS, c * lanes : (c + 1) * lanes
                        ]
                return carry

            return body

        def middle(j, carry):
            def rows(c, h):
                return fields[c, j, h].reshape(2 * per, 4 * lanes)

            even = dot3((ie[0, 0], ie[0, 1]), split_pair(rows(0, 0)))
            other = dot3((ie[1, 0], ie[1, 1]), split_pair(rows(0, 1)))
            odd = dot3(
                (io[0], io[1]), split_pair(jnp.concatenate([rows(1, 0), rows(1, 1)], axis=0))
            )
            re, im = odd[: 2 * per], odd[2 * per :]
            plus, minus = even + other, even - other
            made = []
            for grid in (plus + re, minus - im, plus - re, minus + im):
                u, v, h, w = (grid[:, f * lanes : (f + 1) * lanes] for f in range(4))
                made.append(
                    jnp.concatenate([w * v, w * u, 0.5 * (u * u + v * v), h * u, h * v], axis=1)
                )
            a, b = made[0] + made[2], made[1] + made[3]
            for h, term in enumerate((a + b, a - b)):
                got = dot3((fe[h, 0], fe[h, 1]), split_pair(term))
                modes[slots[0], j, h] = got.reshape(2, kept, 5 * lanes)
            term = jnp.concatenate([made[0] - made[2], made[1] - made[3]], axis=0)
            got = dot3((fo[0], fo[1]), split_pair(term))
            for h in range(2):
                modes[slots[1], j, h] = got[2 * kept * h : 2 * kept * (h + 1)].reshape(
                    2, kept, 5 * lanes
                )
            mode_copy(j).start()
            return carry

        def read(ref, at):
            return tuple(
                tuple(
                    jnp.concatenate([ref[h, f, c, pl.ds(at, 8)] for h in range(2)], axis=0)
                    for c in range(2)
                )
                for f in range(3)
            )

        def write(ref, at, values):
            for f in range(3):
                for c in range(2):
                    for h in range(2):
                        ref[h, f, c, pl.ds(at, 8)] = values[f][c][8 * h : 8 * h + 8]

        def rows_of(i):
            at = pl.multiple_of(i * 8, 8)
            ky = jnp.concatenate([rows_ky(h, at, 8) for h in range(2)], axis=0)
            factors = tuple(
                jnp.concatenate([fac[n, h, pl.ds(at, 8)] for h in range(2)], axis=0) for n in range(3)
            )
            return at, ky, factors

        def plain(i, carry):
            at, ky, factors = rows_of(i)
            write(state, at, apply_parts(read(state, at), factors, kx, ky))
            return carry

        def turn_of(n):
            last = total - (zones - 1) * each
            m = n - last * zones
            others = max(zones - 1, 1)
            early = lax.rem(n, zones) * each + n // zones
            late = lax.rem(m + others, others) * each + last + m // others
            return jnp.where(m < 0, early, late)

        def forward(step):
            def body(n, carry):
                i = n if step == 0 else turn_of(n)
                at, ky, factors = rows_of(i)

                def piece(f, c, k):
                    return jnp.concatenate(
                        [
                            modes[k // half, k % half, h, c, pl.ds(at, 8), f * lanes : (f + 1) * lanes]
                            for h in range(2)
                        ],
                        axis=0,
                    )

                stacked = jnp.concatenate(
                    [
                        jnp.concatenate([piece(f, 0, k), piece(f, 1, k)], axis=1)
                        for f in range(5)
                        for k in range(RADIX)
                    ],
                    axis=0,
                )
                made = dot3(split_pair(stacked), (fx[0], fx[1]))
                found = []
                for f in range(5):
                    parts = []
                    for k in range(RADIX):
                        start = (f * RADIX + k) * 16
                        a = made[start : start + 16, :lanes]
                        b = made[start : start + 16, lanes:]
                        if k > 0:
                            c, s = ftw[0, k : k + 1], ftw[1, k : k + 1]
                            a, b = a * c - b * s, a * s + b * c
                        parts.append((a, b))
                    parts = small_fft(parts, -1.0)
                    found.append(
                        tuple(jnp.concatenate([p[c] for p in parts], axis=1) for c in range(2))
                    )
                (ar, ai), (br, bi), (kr, ki), (pr, pi), (qr, qi) = found
                inside = (jnp.abs(kx) <= limit) & (ky <= limit)

                def keep(values):
                    return jnp.where(inside, dt * values, 0.0)

                change = (
                    (keep(ar + kx * ki), keep(ai - kx * kr)),
                    (keep(ky * ki - br), -keep(bi + ky * kr)),
                    (keep(kx * pi + ky * qi), -keep(kx * pr + ky * qr)),
                )

                def add(left, right):
                    return tuple(tuple(a + b for a, b in zip(p, q)) for p, q in zip(left, right))

                if step == 0:
                    change = apply_parts(change, factors, kx, ky)
                    write(delta, at, change)
                    moved = apply_parts(read(state, at), factors, kx, ky)
                    write(state, at, add(moved, change))
                else:
                    change = add(change, read(delta, at))
                    change = apply_parts(change, factors, kx, ky)
                    for f in range(3):
                        for c in range(2):
                            for h in range(2):
                                value = change[f][c][8 * h : 8 * h + 8]
                                delta[h, f, c, pl.ds(at, 8), :low] = value[:, :low]
                                delta[h, f, c, pl.ds(at, 8), low : 2 * low] = value[:, grid_size - low :]

                    @pl.when(stays(i))
                    def _():
                        to = lax.rem(i, each)
                        for h in range(2):
                            pltpu.make_async_copy(
                                back_part(i, h), off.at[me, to, h], brecv.at[me, to, h]
                            ).start()

                    @pl.when(is_job & jnp.logical_not(stays(i)))
                    def _():
                        for h in range(2):
                            back_copy(i, h).start()

                return carry

            return body

        fillers = (
            inverse_tables,
            forward_tables,
            lambda: fine_factors(0),
            lambda: fine_factors(1),
            scan_factors,
        )
        for n in range(6):
            send_part(n)
            if n < len(fillers):
                fillers[n]()

        def steps():
            for step in range(CF):
                for f in (0, 1, 3, 2):
                    if step == 0 and f < 3:
                        for n in (2 * f, 2 * f + 1):
                            for at in range(group):
                                gather_wait(n, at)
                    for h in range(2):
                        lax.fori_loop(0, blocks, inverse(f, h), 0, unroll=True)
                        field_copy(f, h).start()
                for f in range(4):
                    for h in range(2):
                        field_copy(f, h).wait()
                lax.fori_loop(0, half, middle, 0)
                if step < CF - 1:
                    lax.fori_loop(kept // 8, per // 8, plain, 0)
                for j in range(half):
                    mode_copy(j).wait()
                lax.fori_loop(0, kept // 8, forward(step), 0)

        pl.when(is_job)(steps)

        span = rows // each

        def base_copies():
            pairs = [(i_ref, state.at[0, :, :, :rows]), (c_ref.at[0], state.at[1, :, :, :rows])]
            return [pltpu.make_async_copy(ref, to, bases.at[n]) for n, (ref, to) in enumerate(pairs)]

        def before_copy(ref):
            return pltpu.make_async_copy(ref, fac.at[:, :, :rows], bases.at[2])

        for copy in base_copies():
            copy.start()

        @pl.when(own == 0)
        def _():
            before_copy(i_ref).start()

        @pl.when(own > 0)
        def _():
            before_copy(prev).start()

        for copy in base_copies():
            copy.wait()
        before_copy(prev).wait()

        def base_rows(b, carry):
            at = pl.multiple_of(b * 8, 8)
            row = pl.ds(at, 8)
            m = lax.broadcasted_iota(jnp.int32, (8, 1), 0) + (z * rows + at)
            ky = m.astype(jnp.float32)
            for n, steps in enumerate(((CF * (own + 1)).astype(jnp.float32), float(CF))):
                factors = prop_factors(steps, kx, ky, grid_size)
                start = tuple(
                    tuple(state[0, f, c, row] if n == 0 else fac[f, c, row] for c in range(2))
                    for f in range(3)
                )
                made = apply_parts(start, factors, kx, ky)
                for f in range(3):
                    for c in range(2):
                        if n == 0:
                            state[0, f, c, row] = made[f][c]
                        else:
                            state[1, f, c, row] = made[f][c] - state[1, f, c, row]
            return carry

        lax.fori_loop(0, rows // 8, base_rows, 0)

        def out_copy(n, at):
            row = pl.ds(pl.multiple_of(at * span, 8), span)
            to = (new_out, res_out)[n].at[0, :, :, row]
            return pltpu.make_async_copy(state.at[n, :, :, row], to, osem.at[n, at])

        zone_blocks = jnp.where(is_home, jnp.minimum(each, total - z * each), 0)

        def out_now(at, carry):
            for n in range(2):
                out_copy(n, at).start()
            return carry

        lax.fori_loop(zone_blocks, each, out_now, 0)

        def finish(at):
            row = pl.ds(pl.multiple_of(at * span, 8), span)
            for k, ref in enumerate((sums, off)):
                for f in range(3):
                    for c in range(2):
                        for n in range(2 * low // 128):
                            for side in range(2):
                                for h in range(2):
                                    held[c, n, pl.ds(side + 2 * h, 8, stride=4), :] = ref[
                                        side, at, h, f, c, :, n * 128 : (n + 1) * 128
                                    ]
                            lane = n * 128 if n * 128 < low else grid_size - 2 * low + n * 128
                            lane = slice(lane, lane + 128)
                            state[k, f, c, row, lane] = state[k, f, c, row, lane] + held[c, n, :span]
                out_copy(k, at).start()

        def chunk(ref, side, at, h):
            return tuple(tuple(ref[side, at, h, f, c] for c in range(2)) for f in range(3))

        def moved(n, values, side, at, h):
            m = lax.broadcasted_iota(jnp.int32, (8, 1), 0) + (z * short + at * 8)
            ky = (4 * m + 2 * h + side).astype(jnp.float32)
            factors = tuple(sfac[n, k, side, at, h] for k in range(3))
            return apply_parts(values, factors, kx_low, ky)

        def put(side, at, h, values):
            for f in range(3):
                for c in range(2):
                    sums[side, at, h, f, c] = values[f][c]

        def plus(left, right):
            return tuple(tuple(a + b for a, b in zip(p, q)) for p, q in zip(left, right))

        def landed_copy(side, at, h):
            part = off.at[side, at, h]
            return pltpu.make_async_copy(part, part, brecv.at[side, at, h])

        def pair_copy(side, at, h):
            return pltpu.make_async_remote_copy(
                off.at[side, at, h],
                mates.at[side, at, h],
                psend.at[side, at, h],
                precv.at[side, at, h],
                device_id=(ta, 1, z),
                device_id_type=MESH,
            )

        def share_copy(side, at, h):
            return pltpu.make_async_remote_copy(
                carry_in.at[side, at, h],
                carry_in.at[side, at, h],
                csend.at[side, at, h],
                crecv.at[side, at, h],
                device_id=(ta, 0, z),
                device_id_type=MESH,
            )

        def chain_copy(side, at, h):
            return pltpu.make_async_remote_copy(
                sums.at[side, at, h],
                carry_in.at[side, at, h],
                ssend.at[side, at, h],
                crecv.at[side, at, h],
                device_id=(lax.rem(ta + 1, chips), 1, z),
                device_id_type=MESH,
            )

        def over(body):
            def step(t, carry):
                body(lax.rem(t, 2), t // 4, lax.rem(t // 2, 2))
                return carry

            lax.fori_loop(0, zone_blocks * 4, step, 0)

        def end_group(side, at, h):
            @pl.when(side + h == 2)
            def _():
                finish(at)

        @pl.when(is_home & (me == 0))
        def _():
            def start(side, at, h):
                landed_copy(side, at, h).wait()
                pair_copy(side, at, h).start()

            over(start)

            def rest(side, at, h):
                @pl.when(first)
                def _():
                    put(side, at, h, chunk(off, side, at, h))

                @pl.when(ta > 0)
                def _():
                    share_copy(side, at, h).wait_recv()
                    carried = moved(0, chunk(carry_in, side, at, h), side, at, h)
                    put(side, at, h, plus(chunk(off, side, at, h), carried))

                end_group(side, at, h)

            over(rest)

            def end(side, at, h):
                pair_copy(side, at, h).wait_send()

            over(end)

        @pl.when(is_home & (me == 1))
        def _():
            def step(side, at, h):
                landed_copy(side, at, h).wait()
                pair_copy(side, at, h).wait_recv()
                both = plus(chunk(off, side, at, h), moved(0, chunk(mates, side, at, h), side, at, h))

                @pl.when(first)
                def _():
                    put(side, at, h, both)

                @pl.when(ta > 0)
                def _():
                    chain_copy(side, at, h).wait_recv()
                    share_copy(side, at, h).start()
                    put(side, at, h, plus(both, moved(1, chunk(carry_in, side, at, h), side, at, h)))

                @pl.when(passes_on)
                def _():
                    chain_copy(side, at, h).start()

                end_group(side, at, h)

            over(step)

            def end(side, at, h):
                @pl.when(ta > 0)
                def _():
                    share_copy(side, at, h).wait_send()

                @pl.when(passes_on)
                def _():
                    chain_copy(side, at, h).wait_send()

            over(end)

        for n in range(2):
            for at in range(each):
                out_copy(n, at).wait()

        @pl.when((me == 0) | shifts)
        def _():
            for n in range(6):
                prev_copy(n).wait_send()

        for n in range(6):
            for side in range(2):

                @pl.when(jnp.logical_not((z == own_z) & (me == side)))
                def _():
                    gather_copy(n, side).wait_send()

        @pl.when(is_job)
        def _():
            def end(i, carry):
                @pl.when(jnp.logical_not(stays(i)))
                def _():
                    for h in range(2):
                        back_copy(i, h).wait_send()

                return carry

            lax.fori_loop(0, total, end, 0)

    return pl.pallas_call(
        kernel,
        in_specs=[pl.BlockSpec(memory_space=pl.ANY)] * 2 + [pl.BlockSpec(memory_space=pltpu.VMEM)] * 4,
        out_specs=[pl.BlockSpec(memory_space=pl.ANY)] * 3,
        out_shape=[jax.ShapeDtypeStruct(c_state.shape, jnp.float32)] * 2
        + [jax.ShapeDtypeStruct((3, 2, rows, grid_size), jnp.float32)],
        scratch_shapes=[
            pltpu.VMEM((2, 3, 2, per, grid_size), jnp.float32),
            pltpu.VMEM((3, half, 2, 2, per, 4 * lanes), jnp.float32),
            pltpu.VMEM((3, half, 2, 2, kept, 5 * lanes), jnp.float32),
            pltpu.VMEM((2, 3, 2, kept, grid_size), jnp.float32),
            *[pltpu.VMEM((2, each, 2, 3, 2, 8, 2 * low), jnp.float32)] * 4,
            pltpu.VMEM((3, 2, per, grid_size), jnp.float32),
            pltpu.VMEM((2, 3, 2, each, 2, 8, 2 * low), jnp.float32),
            pltpu.VMEM((2, 2, quarter, quarter), jnp.bfloat16),
            pltpu.VMEM((2, 2 * quarter, 2 * quarter), jnp.bfloat16),
            pltpu.VMEM((2, 2, 2 * kept, quarter), jnp.bfloat16),
            pltpu.VMEM((2, 4 * kept, 2 * quarter), jnp.bfloat16),
            pltpu.VMEM((2, grid_size // 128, rows, 128), jnp.float32),
            pltpu.VMEM((6, 2, 2, short, grid_size), jnp.float32),
            pltpu.SemaphoreType.DMA((2, grid_size // 128)),
            pltpu.SemaphoreType.DMA((6,)),
            pltpu.SemaphoreType.DMA((6,)),
            pltpu.SemaphoreType.DMA((6, 2)),
            pltpu.SemaphoreType.DMA((6, group)),
            pltpu.SemaphoreType.DMA((3,)),
            pltpu.SemaphoreType.DMA((4, 2)),
            pltpu.SemaphoreType.DMA((4, 2)),
            pltpu.SemaphoreType.DMA((half,)),
            pltpu.SemaphoreType.DMA((half,)),
            pltpu.SemaphoreType.DMA((total, 2)),
            *[pltpu.SemaphoreType.DMA((2, each, 2))] * 6,
            pltpu.SemaphoreType.DMA((2, each)),
        ],
        compiler_params=pltpu.CompilerParams(
            collective_id=0, has_side_effects=True, vmem_limit_bytes=63 * 1024 * 1024
        ),
        name="fine_steps",
    )(c_state, init, inv_x, inv_tw, fwd_x, fwd_tw)


def shards(c_state, init):
    group = lax.axis_size(SPACE)
    slabs = lax.axis_size(SLAB)
    where = (group // 2 - 1, group // 2)
    return tuple(fine_steps(c_state, init, slabs, group, where)[:2])


def solution(mesh):
    slabs, space = mesh.devices.shape
    fine = Mesh(mesh.devices.reshape(slabs // 2, 2, space), EVERY)
    spec = P(SLAB, None, None, SPACE, None)
    return jax.shard_map(
        shards,
        mesh=fine,
        in_specs=(spec, P(None, None, SPACE, None)),
        out_specs=(spec, spec),
        check_vma=False,
    )
```

```python
import math

import jax
import jax.numpy as jnp
import numpy as np
from jax import lax
from jax.experimental import pallas as pl
from jax.experimental.pallas import tpu as pltpu
from jax.sharding import Mesh, PartitionSpec as P

CF = 2
CORIOLIS = 1.0
HYPERDIFFUSION = 0.25
COURANT = 0.4
RADIX = 8
ROWS = 32
SLAB = ("ta", "core")
SPACE = "sp"
EVERY = ("ta", "core", "sp")


def split_pair(values):
    high = values.astype(jnp.bfloat16)
    return high, (values - high.astype(jnp.float32)).astype(jnp.bfloat16)


def table_pair(values):
    high = lax.reduce_precision(values, 8, 7)
    return jnp.stack([high, values - high], axis=-3).astype(jnp.bfloat16)


def dot3(left, right):
    def one(a, b):
        return jnp.dot(a, b, preferred_element_type=jnp.float32)

    return one(left[0], right[0]) + (one(left[0], right[1]) + one(left[1], right[0]))


def small_fft(parts, sign):
    count = len(parts)
    if count == 1:
        return parts
    even = small_fft(parts[0::2], sign)
    odd = small_fft(parts[1::2], sign)
    low, high = [], []
    for k in range(count // 2):
        re, im = odd[k]
        if k == 0:
            tr, ti = re, im
        elif 4 * k == count:
            tr, ti = (-im, re) if sign > 0 else (im, -re)
        else:
            c = math.cos(2.0 * math.pi * k / count)
            s = sign * math.sin(2.0 * math.pi * k / count)
            tr, ti = re * c - im * s, re * s + im * c
        low.append((even[k][0] + tr, even[k][1] + ti))
        high.append((even[k][0] - tr, even[k][1] - ti))
    return low + high


def lane_tables(grid_size, sign):
    lanes = grid_size // RADIX
    n = np.arange(lanes)
    angle = 2.0 * np.pi * (n[:, None] * n[None, :] % lanes) / lanes
    c, s = np.cos(angle), sign * np.sin(angle)
    full = np.block([[c, s], [-s, c]]).astype(np.float32)
    high = full.astype(jnp.bfloat16)
    low = (full - high.astype(np.float32)).astype(jnp.bfloat16)
    turn = 2.0 * np.pi * (np.arange(RADIX)[:, None] * n[None, :]) / grid_size
    twiddle = np.stack([np.cos(turn), sign * np.sin(turn)]).astype(np.float32)
    return jnp.asarray(np.stack([high, low])), jnp.asarray(twiddle)


def prop_factors(steps, wave_x, wave_y, grid_size):
    time_step = COURANT / grid_size
    squared = wave_x * wave_x + wave_y * wave_y
    frequency = jnp.sqrt(CORIOLIS * CORIOLIS + squared)
    ratio = squared / (0.25 * grid_size * grid_size)
    log_damp = -HYPERDIFFUSION * (ratio * ratio) * (ratio * ratio)
    phase_angle = frequency * (steps * time_step)
    first_coef = jnp.sin(phase_angle) / frequency
    second_coef = (1.0 - jnp.cos(phase_angle)) / (frequency * frequency)
    damping = jnp.exp(steps * log_damp)
    return first_coef, second_coef, damping


def apply_parts(state, factors, kx, ky):
    first, second, damp = factors
    (xr, xi), (yr, yi), (hr, hi) = state
    done = []
    for x, y, p in ((xr, yr, -hi), (xi, yi, hr)):
        m1 = CORIOLIS * y - kx * p
        m2 = -CORIOLIS * x - ky * p
        m3 = kx * x + ky * y
        n1 = CORIOLIS * m2 - kx * m3
        n2 = -CORIOLIS * m1 - ky * m3
        n3 = kx * m1 + ky * m2
        done.append(
            (
                (x + first * m1 + second * n1) * damp,
                (y + first * m2 + second * n2) * damp,
                (p + first * m3 + second * n3) * damp,
            )
        )
    real, imag = done
    return ((real[0], imag[0]), (real[1], imag[1]), (imag[2], -real[2]))


def fine_steps(c_state, init, slabs, group, where):
    chips = slabs // 2
    MESH = pl.DeviceIdType.MESH
    rows, grid_size = c_state.shape[3:]
    short = rows // 4
    third = grid_size // 3
    kept = -(-(third // 4 + 1) // 8) * 8
    low = (third // 128 + 1) * 128
    per = grid_size // 8
    quarter = grid_size // 4
    lanes = grid_size // RADIX
    half = RADIX // 2
    blocks = per // ROWS
    limit = float(third)
    zones = -(-(third + 1) // rows)
    dt = COURANT / grid_size
    total = kept // 8
    each = short // 8
    inv_x, inv_tw = lane_tables(grid_size, 1.0)
    fwd_x, fwd_tw = lane_tables(grid_size, -1.0)

    def kernel(*refs):
        c_ref, i_ref, ix, itw, fx, ftw, new_out, res_out, prev = refs[:9]
        state, fields, modes, delta, off, mates, carry_in, sums = refs[9:17]
        fac, sfac, ie, io, fe, fo, held, dealt, winds = refs[17:26]
        load, vsend, vrecv, gsend, grecv, bases = refs[26:32]
        fsend, frecv, msend, mrecv, bsend, brecv, psend, precv, csend, crecv, ssend, osem = refs[32:]
        ta, me, z = (lax.axis_index(name) for name in EVERY)
        mate = (ta, 1 - me, z)
        which = jnp.where(z == where[1], 1, 0)
        is_job = (z == where[0]) | (z == where[1])
        is_home = z < zones
        first = ta == 0
        shifts = (me == 1) & (ta < chips - 1)
        passes_on = shifts & is_home
        own_z = jnp.where(me == 1, where[1], where[0])
        own = 2 * ta + me
        home_is_own = is_job & is_home & (which == me)
        kx = lax.broadcasted_iota(jnp.int32, (1, grid_size), 1)
        kx = jnp.where(kx < grid_size // 2, kx, kx - grid_size).astype(jnp.float32)
        kx_low = jnp.concatenate([kx[:, :low], kx[:, grid_size - low :]], axis=1)
        slots = (2 * me, 2 - me)
        seat = (0, 1, 3, 2)

        barrier = pltpu.get_barrier_semaphore()
        pl.semaphore_signal(barrier, inc=1, device_id=mate, device_id_type=MESH)
        for side in range(2):

            @pl.when(is_home & jnp.logical_not((z == own_z) & (me == side)))
            def _():
                pl.semaphore_signal(barrier, inc=1, device_id=(ta, side, own_z), device_id_type=MESH)

        for at in range(group):

            @pl.when(is_job & jnp.logical_not((z == at) & (me == which)))
            def _():
                pl.semaphore_signal(barrier, inc=1, device_id=(ta, which, at), device_id_type=MESH)

        @pl.when((me == 0) & (ta > 0))
        def _():
            pl.semaphore_signal(barrier, inc=1, device_id=(ta - 1, 1, z), device_id_type=MESH)

        @pl.when(is_home & (me == 1) & (ta > 0))
        def _():
            pl.semaphore_signal(barrier, inc=1, device_id=(ta - 1, 1, z), device_id_type=MESH)

        expected = (
            3
            + jnp.where(shifts, 1, 0)
            + jnp.where(passes_on, 1, 0)
            - jnp.where(z == own_z, 1, 0)
            + jnp.where(is_job, zones, 0)
            - jnp.where(home_is_own, 1, 0)
        )
        pl.semaphore_wait(barrier, expected)

        def prev_copy(n):
            f, c = n // 2, n % 2
            return pltpu.make_async_remote_copy(
                c_ref.at[0, f, c],
                prev.at[f, c],
                vsend.at[n],
                vrecv.at[n],
                device_id=(jnp.where(me == 1, lax.rem(ta + 1, chips), ta), 1 - me, z),
                device_id_type=MESH,
            )

        def state_part(n):
            return state.at[:, n // 2, n % 2, pl.ds(pl.multiple_of(z * short, 8), short)]

        def gather_copy(n, side):
            return pltpu.make_async_remote_copy(
                dealt.at[n, side],
                state_part(n),
                gsend.at[n, side],
                grecv.at[n, z],
                device_id=(ta, side, own_z),
                device_id_type=MESH,
            )

        def gather_wait(n, at):
            row = pl.ds(at * short, short)
            part = state.at[:, n // 2, n % 2, row]
            pltpu.make_async_copy(part, part, grecv.at[n, at]).wait()

        @pl.when((me == 0) | shifts)
        def _():
            for n in range(6):
                prev_copy(n).start()

        tiles = grid_size // 128

        def fetch(ref, n):
            copies = [
                pltpu.make_async_copy(
                    ref.at[n // 2, n % 2, :, pl.ds(at * 128, 128)], held.at[n % 2, at], load.at[n % 2, at]
                )
                for at in range(tiles)
            ]
            for copy in copies:
                copy.start()
            for copy in copies:
                copy.wait()

        def send_part(n):
            @pl.when(own == 0)
            def _():
                fetch(i_ref, n)

            @pl.when(own > 0)
            def _():
                pltpu.make_async_copy(prev.at[n // 2, n % 2], prev.at[n // 2, n % 2], vrecv.at[n]).wait()
                fetch(prev, n)

            for q in range(4):
                for at in range(tiles):
                    dealt[n, q % 2, q // 2, :, at * 128 : (at + 1) * 128] = held[
                        n % 2, at, pl.ds(q, short, stride=4), :
                    ]
            for side in range(2):
                here = (z == own_z) & (me == side)

                @pl.when(here)
                def _():
                    pltpu.make_async_copy(dealt.at[n, side], state_part(n), grecv.at[n, z]).start()

                @pl.when(jnp.logical_not(here))
                def _():
                    gather_copy(n, side).start()

        def waves(turns):
            angle = 2.0 * math.pi / grid_size * (turns & (grid_size - 1)).astype(jnp.float32)
            return jnp.cos(angle) / grid_size, jnp.sin(angle) / grid_size

        def put_pair(ref, lead, row, lane, values):
            for part, value in enumerate(split_pair(values)):
                ref[(*lead, part, row, lane)] = value

        def inverse_tables():
            for q in range(4):
                for at in range(0, quarter, 64):
                    y = lax.broadcasted_iota(jnp.int32, (64, per), 0) + at
                    ky = 4 * lax.broadcasted_iota(jnp.int32, (64, per), 1) + q
                    c, s = waves(y * ky)
                    weight = jnp.where(ky == 0, 1.0, 2.0)
                    c, s = c * weight, s * weight
                    row, next_row = slice(at, at + 64), slice(quarter + at, quarter + at + 64)
                    if q % 2 == 0:
                        put_pair(ie, (q // 2,), row, slice(0, per), c)
                        put_pair(ie, (q // 2,), row, slice(per, 2 * per), -s)
                    else:
                        base = (q // 2) * 2 * per
                        sign = 1.0 if q == 1 else -1.0
                        put_pair(io, (), row, slice(base, base + per), c)
                        put_pair(io, (), row, slice(base + per, base + 2 * per), -s)
                        put_pair(io, (), next_row, slice(base, base + per), sign * s)
                        put_pair(io, (), next_row, slice(base + per, base + 2 * per), sign * c)

        def forward_tables():
            for q in range(4):
                y = lax.broadcasted_iota(jnp.int32, (kept, quarter), 1)
                ky = 4 * lax.broadcasted_iota(jnp.int32, (kept, quarter), 0) + q
                c, s = waves(y * ky)
                if q % 2 == 0:
                    both = jnp.concatenate([c, -s], axis=0)
                    put_pair(fe, (q // 2,), slice(None), slice(None), both)
                else:
                    sign = 1.0 if q == 1 else -1.0
                    both = jnp.concatenate(
                        [
                            jnp.concatenate([c, -sign * s], axis=1),
                            jnp.concatenate([-s, -sign * c], axis=1),
                        ],
                        axis=0,
                    )
                    base = (q // 2) * 2 * kept
                    put_pair(fo, (), slice(base, base + 2 * kept), slice(None), both)

        def fine_factors(h):
            def body(b, carry):
                at = pl.multiple_of(b * 16, 16)
                made = prop_factors(1.0, kx, rows_ky(h, at, 16), grid_size)
                for n in range(3):
                    fac[n, h, pl.ds(at, 16)] = made[n]
                return carry

            lax.fori_loop(0, per // 16, body, 0)

        def scan_factors():
            def body(b, carry):
                at = b // 4
                side, h = b // 2 % 2, b % 2
                m = lax.broadcasted_iota(jnp.int32, (8, 1), 0) + (z * short + at * 8)
                ky = (4 * m + 2 * h + side).astype(jnp.float32)
                for k in range(2):
                    made = prop_factors(float(CF * (k + 1)), kx_low, ky, grid_size)
                    for n in range(3):
                        sfac[k, n, side, at, h] = made[n]
                return carry

            lax.fori_loop(0, 4 * each, body, 0)

        def back_part(i, h):
            return delta.at[h, :, :, pl.ds(pl.multiple_of(i * 8, 8), 8), : 2 * low]

        def back_copy(i, h):
            return pltpu.make_async_remote_copy(
                back_part(i, h),
                off.at[me, lax.rem(i, each), h],
                bsend.at[i, h],
                brecv.at[me, lax.rem(i, each), h],
                device_id=(ta, which, i // each),
                device_id_type=MESH,
            )

        def stays(i):
            return home_is_own & (i // each == z)

        def field_copy(f, h):
            lane = slice(seat[f] * lanes, (seat[f] + 1) * lanes)
            return pltpu.make_async_remote_copy(
                fields.at[2, :, h, :, :, lane],
                fields.at[me, :, h, :, :, lane],
                fsend.at[f, h],
                frecv.at[f, h],
                device_id=mate,
                device_id_type=MESH,
            )

        def mode_copy(j, part):
            lane = slice(0, 3 * lanes) if part == 0 else slice(3 * lanes, 5 * lanes)
            return pltpu.make_async_remote_copy(
                modes.at[2, j, :, :, :, lane],
                modes.at[me, j, :, :, :, lane],
                msend.at[j, part],
                mrecv.at[j, part],
                device_id=mate,
                device_id_type=pl.DeviceIdType.MESH,
            )

        def rows_ky(h, at, count):
            m = lax.broadcasted_iota(jnp.int32, (count, 1), 0) + at
            return (4 * m + 2 * h + me).astype(jnp.float32)

        def inverse(f, h):
            def body(b, carry):
                at = pl.multiple_of(b * ROWS, ROWS)
                row = pl.ds(at, ROWS)
                if f < 3:
                    re, im = state[h, f, 0, row], state[h, f, 1, row]
                else:
                    ky = rows_ky(h, at, ROWS)
                    re = ky * state[h, 0, 1, row] - kx * state[h, 1, 1, row]
                    im = kx * state[h, 1, 0, row] - ky * state[h, 0, 0, row]
                parts = [
                    (re[:, n * lanes : (n + 1) * lanes], im[:, n * lanes : (n + 1) * lanes])
                    for n in range(RADIX)
                ]
                turned = []
                for k, (a, b_) in enumerate(small_fft(parts, 1.0)):
                    if k > 0:
                        c, s = itw[0, k : k + 1], itw[1, k : k + 1]
                        a, b_ = a * c - b_ * s, a * s + b_ * c
                    turned.append(jnp.concatenate([a, b_], axis=1))
                made = dot3(split_pair(jnp.concatenate(turned, axis=0)), (ix[0], ix[1]))
                for k in range(RADIX):
                    for c in range(2):
                        fields[
                            slots[k // half], k % half, h, c, row, seat[f] * lanes : (seat[f] + 1) * lanes
                        ] = made[
                            k * ROWS : (k + 1) * ROWS, c * lanes : (c + 1) * lanes
                        ]
                return carry

            return body

        def middle(part):
            lane = (slice(0, 3 * lanes), slice(3 * lanes, 4 * lanes), slice(0, 4 * lanes))[part]
            to = (slice(0, 3 * lanes), slice(3 * lanes, 5 * lanes), slice(0, 5 * lanes))[part]
            width = to.stop - to.start

            def body(j, carry):
                def side(c, h):
                    return fields[c, j, h, :, :, lane].reshape(2 * per, lane.stop - lane.start)

                even = dot3((ie[0, 0], ie[0, 1]), split_pair(side(0, 0)))
                other = dot3((ie[1, 0], ie[1, 1]), split_pair(side(0, 1)))
                odd = dot3(
                    (io[0], io[1]), split_pair(jnp.concatenate([side(1, 0), side(1, 1)], axis=0))
                )
                re, im = odd[: 2 * per], odd[2 * per :]
                plus, minus = even + other, even - other
                made = []
                for n, grid in enumerate((plus + re, minus - im, plus - re, minus + im)):
                    parts = [grid[:, f : f + lanes] for f in range(0, grid.shape[1], lanes)]
                    products = []
                    if part == 1:
                        u, v = winds[j, n, :, :lanes], winds[j, n, :, lanes:]
                    else:
                        u, v, w = parts[:3]
                        products += [w * v, w * u, 0.5 * (u * u + v * v)]
                    if part == 0:
                        winds[j, n] = grid[:, : 2 * lanes]
                    else:
                        products += [parts[-1] * u, parts[-1] * v]
                    made.append(jnp.concatenate(products, axis=1))
                a, b = made[0] + made[2], made[1] + made[3]
                for h, term in enumerate((a + b, a - b)):
                    got = dot3((fe[h, 0], fe[h, 1]), split_pair(term))
                    modes[slots[0], j, h, :, :, to] = got.reshape(2, kept, width)
                term = jnp.concatenate([made[0] - made[2], made[1] - made[3]], axis=0)
                got = dot3((fo[0], fo[1]), split_pair(term))
                for h in range(2):
                    modes[slots[1], j, h, :, :, to] = got[2 * kept * h : 2 * kept * (h + 1)].reshape(
                        2, kept, width
                    )
                for n in (0, 1):
                    if part in (n, 2):
                        mode_copy(j, n).start()
                return carry

            return body

        def read(ref, at, count=3):
            return tuple(
                tuple(
                    jnp.concatenate([ref[h, f, c, pl.ds(at, 8)] for h in range(2)], axis=0)
                    for c in range(2)
                )
                for f in range(count)
            )

        def write(ref, at, values):
            for f in range(len(values)):
                for c in range(2):
                    for h in range(2):
                        ref[h, f, c, pl.ds(at, 8)] = values[f][c][8 * h : 8 * h + 8]

        def rows_of(i):
            at = pl.multiple_of(i * 8, 8)
            ky = jnp.concatenate([rows_ky(h, at, 8) for h in range(2)], axis=0)
            factors = tuple(
                jnp.concatenate([fac[n, h, pl.ds(at, 8)] for h in range(2)], axis=0) for n in range(3)
            )
            return at, ky, factors

        def plain(i, carry):
            at, ky, factors = rows_of(i)
            write(state, at, apply_parts(read(state, at), factors, kx, ky))
            return carry

        def turn_of(n):
            last = total - (zones - 1) * each
            m = n - last * zones
            others = max(zones - 1, 1)
            early = lax.rem(n, zones) * each + n // zones
            late = lax.rem(m + others, others) * each + last + m // others
            return jnp.where(m < 0, early, late)

        def forward(step, part):
            which_fields = ((0, 1, 2), (3, 4), (0, 1, 2, 3, 4))[part]

            def body(n, carry):
                i = n if step == 0 else turn_of(n)
                at, ky, factors = rows_of(i)

                def piece(f, c, k):
                    return jnp.concatenate(
                        [
                            modes[k // half, k % half, h, c, pl.ds(at, 8), f * lanes : (f + 1) * lanes]
                            for h in range(2)
                        ],
                        axis=0,
                    )

                stacked = jnp.concatenate(
                    [
                        jnp.concatenate([piece(f, 0, k), piece(f, 1, k)], axis=1)
                        for f in which_fields
                        for k in range(RADIX)
                    ],
                    axis=0,
                )
                made = dot3(split_pair(stacked), (fx[0], fx[1]))
                found = []
                for f in range(len(which_fields)):
                    parts = []
                    for k in range(RADIX):
                        start = (f * RADIX + k) * 16
                        a = made[start : start + 16, :lanes]
                        b = made[start : start + 16, lanes:]
                        if k > 0:
                            c, s = ftw[0, k : k + 1], ftw[1, k : k + 1]
                            a, b = a * c - b * s, a * s + b * c
                        parts.append((a, b))
                    parts = small_fft(parts, -1.0)
                    found.append(
                        tuple(jnp.concatenate([p[c] for p in parts], axis=1) for c in range(2))
                    )
                inside = (jnp.abs(kx) <= limit) & (ky <= limit)

                def keep(values):
                    return jnp.where(inside, dt * values, 0.0)

                if part == 1:
                    change = read(delta, at, 2)
                else:
                    (ar, ai), (br, bi), (kr, ki) = found[:3]
                    change = (
                        (keep(ar + kx * ki), keep(ai - kx * kr)),
                        (keep(ky * ki - br), -keep(bi + ky * kr)),
                    )
                if part == 0:
                    write(delta, at, change)
                    return carry
                (pr, pi), (qr, qi) = found[-2:]
                change = (*change, (keep(kx * pi + ky * qi), -keep(kx * pr + ky * qr)))

                def add(left, right):
                    return tuple(tuple(a + b for a, b in zip(p, q)) for p, q in zip(left, right))

                if step == 0:
                    change = apply_parts(change, factors, kx, ky)
                    write(delta, at, change)
                    moved = apply_parts(read(state, at), factors, kx, ky)
                    write(state, at, add(moved, change))
                else:
                    change = add(change, read(delta, at))
                    change = apply_parts(change, factors, kx, ky)
                    for f in range(3):
                        for c in range(2):
                            for h in range(2):
                                value = change[f][c][8 * h : 8 * h + 8]
                                delta[h, f, c, pl.ds(at, 8), :low] = value[:, :low]
                                delta[h, f, c, pl.ds(at, 8), low : 2 * low] = value[:, grid_size - low :]

                    @pl.when(stays(i))
                    def _():
                        to = lax.rem(i, each)
                        for h in range(2):
                            pltpu.make_async_copy(
                                back_part(i, h), off.at[me, to, h], brecv.at[me, to, h]
                            ).start()

                    @pl.when(is_job & jnp.logical_not(stays(i)))
                    def _():
                        for h in range(2):
                            back_copy(i, h).start()

                return carry

            return body

        fillers = (
            inverse_tables,
            forward_tables,
            lambda: fine_factors(0),
            lambda: fine_factors(1),
            scan_factors,
        )
        for n in range(6):
            send_part(n)
            if n < len(fillers):
                fillers[n]()

        def steps():
            def columns(f):
                for h in range(2):
                    lax.fori_loop(0, blocks, inverse(f, h), 0, unroll=True)
                    field_copy(f, h).start()

            def columns_wait(f):
                for h in range(2):
                    field_copy(f, h).wait()

            def modes_wait(part):
                for j in range(half):
                    mode_copy(j, part).wait()

            def arrived(f):
                for n in (2 * f, 2 * f + 1):
                    for at in range(group):
                        gather_wait(n, at)

            for f in (0, 1):
                arrived(f)
                columns(f)
            columns(3)
            for f in (0, 1, 3):
                columns_wait(f)
            lax.fori_loop(0, half, middle(0), 0)
            modes_wait(0)
            lax.fori_loop(0, kept // 8, forward(0, 0), 0)
            arrived(2)
            columns(2)
            columns_wait(2)
            lax.fori_loop(0, half, middle(1), 0)
            lax.fori_loop(kept // 8, per // 8, plain, 0)
            modes_wait(1)
            lax.fori_loop(0, kept // 8, forward(0, 1), 0)
            for step in range(1, CF):
                for f in (0, 1, 3, 2):
                    columns(f)
                for f in (0, 1, 3, 2):
                    columns_wait(f)
                lax.fori_loop(0, half, middle(2), 0)
                modes_wait(0)
                modes_wait(1)
                lax.fori_loop(0, kept // 8, forward(step, 2), 0)

        pl.when(is_job)(steps)

        span = rows // each

        def base_copies():
            pairs = [(i_ref, state.at[0, :, :, :rows]), (c_ref.at[0], state.at[1, :, :, :rows])]
            return [pltpu.make_async_copy(ref, to, bases.at[n]) for n, (ref, to) in enumerate(pairs)]

        def before_copy(ref):
            return pltpu.make_async_copy(ref, fac.at[:, :, :rows], bases.at[2])

        for copy in base_copies():
            copy.start()

        @pl.when(own == 0)
        def _():
            before_copy(i_ref).start()

        @pl.when(own > 0)
        def _():
            before_copy(prev).start()

        for copy in base_copies():
            copy.wait()
        before_copy(prev).wait()

        def base_rows(b, carry):
            at = pl.multiple_of(b * 8, 8)
            row = pl.ds(at, 8)
            m = lax.broadcasted_iota(jnp.int32, (8, 1), 0) + (z * rows + at)
            ky = m.astype(jnp.float32)
            for n, steps in enumerate(((CF * (own + 1)).astype(jnp.float32), float(CF))):
                factors = prop_factors(steps, kx, ky, grid_size)
                start = tuple(
                    tuple(state[0, f, c, row] if n == 0 else fac[f, c, row] for c in range(2))
                    for f in range(3)
                )
                made = apply_parts(start, factors, kx, ky)
                for f in range(3):
                    for c in range(2):
                        if n == 0:
                            state[0, f, c, row] = made[f][c]
                        else:
                            state[1, f, c, row] = made[f][c] - state[1, f, c, row]
            return carry

        lax.fori_loop(0, rows // 8, base_rows, 0)

        def out_copy(n, at):
            row = pl.ds(pl.multiple_of(at * span, 8), span)
            to = (new_out, res_out)[n].at[0, :, :, row]
            return pltpu.make_async_copy(state.at[n, :, :, row], to, osem.at[n, at])

        zone_blocks = jnp.where(is_home, jnp.minimum(each, total - z * each), 0)

        def out_now(at, carry):
            for n in range(2):
                out_copy(n, at).start()
            return carry

        lax.fori_loop(zone_blocks, each, out_now, 0)

        def finish(at):
            row = pl.ds(pl.multiple_of(at * span, 8), span)
            for k, ref in enumerate((sums, off)):
                for f in range(3):
                    for c in range(2):
                        for n in range(2 * low // 128):
                            for side in range(2):
                                for h in range(2):
                                    held[c, n, pl.ds(side + 2 * h, 8, stride=4), :] = ref[
                                        side, at, h, f, c, :, n * 128 : (n + 1) * 128
                                    ]
                            lane = n * 128 if n * 128 < low else grid_size - 2 * low + n * 128
                            lane = slice(lane, lane + 128)
                            state[k, f, c, row, lane] = state[k, f, c, row, lane] + held[c, n, :span]
                out_copy(k, at).start()

        def chunk(ref, side, at, h):
            return tuple(tuple(ref[side, at, h, f, c] for c in range(2)) for f in range(3))

        def moved(n, values, side, at, h):
            m = lax.broadcasted_iota(jnp.int32, (8, 1), 0) + (z * short + at * 8)
            ky = (4 * m + 2 * h + side).astype(jnp.float32)
            factors = tuple(sfac[n, k, side, at, h] for k in range(3))
            return apply_parts(values, factors, kx_low, ky)

        def put(side, at, h, values):
            for f in range(3):
                for c in range(2):
                    sums[side, at, h, f, c] = values[f][c]

        def plus(left, right):
            return tuple(tuple(a + b for a, b in zip(p, q)) for p, q in zip(left, right))

        def landed_copy(side, at, h):
            part = off.at[side, at, h]
            return pltpu.make_async_copy(part, part, brecv.at[side, at, h])

        def pair_copy(side, at, h):
            return pltpu.make_async_remote_copy(
                off.at[side, at, h],
                mates.at[side, at, h],
                psend.at[side, at, h],
                precv.at[side, at, h],
                device_id=(ta, 1, z),
                device_id_type=MESH,
            )

        def share_copy(side, at, h):
            return pltpu.make_async_remote_copy(
                carry_in.at[side, at, h],
                carry_in.at[side, at, h],
                csend.at[side, at, h],
                crecv.at[side, at, h],
                device_id=(ta, 0, z),
                device_id_type=MESH,
            )

        def chain_copy(side, at, h):
            return pltpu.make_async_remote_copy(
                sums.at[side, at, h],
                carry_in.at[side, at, h],
                ssend.at[side, at, h],
                crecv.at[side, at, h],
                device_id=(lax.rem(ta + 1, chips), 1, z),
                device_id_type=MESH,
            )

        def over(body):
            def step(t, carry):
                body(lax.rem(t, 2), t // 4, lax.rem(t // 2, 2))
                return carry

            lax.fori_loop(0, zone_blocks * 4, step, 0)

        def end_group(side, at, h):
            @pl.when(side + h == 2)
            def _():
                finish(at)

        @pl.when(is_home & (me == 0))
        def _():
            def start(side, at, h):
                landed_copy(side, at, h).wait()
                pair_copy(side, at, h).start()

            over(start)

            def rest(side, at, h):
                @pl.when(first)
                def _():
                    put(side, at, h, chunk(off, side, at, h))

                @pl.when(ta > 0)
                def _():
                    share_copy(side, at, h).wait_recv()
                    carried = moved(0, chunk(carry_in, side, at, h), side, at, h)
                    put(side, at, h, plus(chunk(off, side, at, h), carried))

                end_group(side, at, h)

            over(rest)

            def end(side, at, h):
                pair_copy(side, at, h).wait_send()

            over(end)

        @pl.when(is_home & (me == 1))
        def _():
            def step(side, at, h):
                landed_copy(side, at, h).wait()
                pair_copy(side, at, h).wait_recv()
                both = plus(chunk(off, side, at, h), moved(0, chunk(mates, side, at, h), side, at, h))

                @pl.when(first)
                def _():
                    put(side, at, h, both)

                @pl.when(ta > 0)
                def _():
                    chain_copy(side, at, h).wait_recv()
                    share_copy(side, at, h).start()
                    put(side, at, h, plus(both, moved(1, chunk(carry_in, side, at, h), side, at, h)))

                @pl.when(passes_on)
                def _():
                    chain_copy(side, at, h).start()

                end_group(side, at, h)

            over(step)

            def end(side, at, h):
                @pl.when(ta > 0)
                def _():
                    share_copy(side, at, h).wait_send()

                @pl.when(passes_on)
                def _():
                    chain_copy(side, at, h).wait_send()

            over(end)

        for n in range(2):
            for at in range(each):
                out_copy(n, at).wait()

        @pl.when((me == 0) | shifts)
        def _():
            for n in range(6):
                prev_copy(n).wait_send()

        for n in range(6):
            for side in range(2):

                @pl.when(jnp.logical_not((z == own_z) & (me == side)))
                def _():
                    gather_copy(n, side).wait_send()

        @pl.when(is_job)
        def _():
            def end(i, carry):
                @pl.when(jnp.logical_not(stays(i)))
                def _():
                    for h in range(2):
                        back_copy(i, h).wait_send()

                return carry

            lax.fori_loop(0, total, end, 0)

    return pl.pallas_call(
        kernel,
        in_specs=[pl.BlockSpec(memory_space=pl.ANY)] * 2 + [pl.BlockSpec(memory_space=pltpu.VMEM)] * 4,
        out_specs=[pl.BlockSpec(memory_space=pl.ANY)] * 3,
        out_shape=[jax.ShapeDtypeStruct(c_state.shape, jnp.float32)] * 2
        + [jax.ShapeDtypeStruct((3, 2, rows, grid_size), jnp.float32)],
        scratch_shapes=[
            pltpu.VMEM((2, 3, 2, per, grid_size), jnp.float32),
            pltpu.VMEM((3, half, 2, 2, per, 4 * lanes), jnp.float32),
            pltpu.VMEM((3, half, 2, 2, kept, 5 * lanes), jnp.float32),
            pltpu.VMEM((2, 3, 2, kept, grid_size), jnp.float32),
            *[pltpu.VMEM((2, each, 2, 3, 2, 8, 2 * low), jnp.float32)] * 4,
            pltpu.VMEM((3, 2, per, grid_size), jnp.float32),
            pltpu.VMEM((2, 3, 2, each, 2, 8, 2 * low), jnp.float32),
            pltpu.VMEM((2, 2, quarter, quarter), jnp.bfloat16),
            pltpu.VMEM((2, 2 * quarter, 2 * quarter), jnp.bfloat16),
            pltpu.VMEM((2, 2, 2 * kept, quarter), jnp.bfloat16),
            pltpu.VMEM((2, 4 * kept, 2 * quarter), jnp.bfloat16),
            pltpu.VMEM((2, grid_size // 128, rows, 128), jnp.float32),
            pltpu.VMEM((6, 2, 2, short, grid_size), jnp.float32),
            pltpu.VMEM((half, 4, quarter, 2 * lanes), jnp.float32),
            pltpu.SemaphoreType.DMA((2, grid_size // 128)),
            pltpu.SemaphoreType.DMA((6,)),
            pltpu.SemaphoreType.DMA((6,)),
            pltpu.SemaphoreType.DMA((6, 2)),
            pltpu.SemaphoreType.DMA((6, group)),
            pltpu.SemaphoreType.DMA((3,)),
            pltpu.SemaphoreType.DMA((4, 2)),
            pltpu.SemaphoreType.DMA((4, 2)),
            pltpu.SemaphoreType.DMA((half, 2)),
            pltpu.SemaphoreType.DMA((half, 2)),
            pltpu.SemaphoreType.DMA((total, 2)),
            *[pltpu.SemaphoreType.DMA((2, each, 2))] * 6,
            pltpu.SemaphoreType.DMA((2, each)),
        ],
        compiler_params=pltpu.CompilerParams(
            collective_id=0, has_side_effects=True, vmem_limit_bytes=67043328
        ),
        name="fine_steps",
    )(c_state, init, inv_x, inv_tw, fwd_x, fwd_tw)


def shards(c_state, init):
    group = lax.axis_size(SPACE)
    slabs = lax.axis_size(SLAB)
    where = (group // 2 - 1, group // 2)
    return tuple(fine_steps(c_state, init, slabs, group, where)[:2])


def solution(mesh):
    slabs, space = mesh.devices.shape
    fine = Mesh(mesh.devices.reshape(slabs // 2, 2, space), EVERY)
    spec = P(SLAB, None, None, SPACE, None)
    return jax.shard_map(
        shards,
        mesh=fine,
        in_specs=(spec, P(None, None, SPACE, None)),
        out_specs=(spec, spec),
        check_vma=False,
    )
```
